256 devices in a mesh: row: 8 (over y, z_hi), col: 32 (over z_lo, x, core).
Axes of the slice: x: 4, y: 4, z: 8 (z_hi: 2, z_lo: 4; z = z_hi * 4 + z_lo), core: 2. Of those that a mesh axis runs over, the one named last changes fastest.
Arguments:
- embedding: bfloat16 [98304, 256], P(('col', 'row')), may hold values from -6 to 6
- weight: bfloat16 [256, 256], replicated, may hold values from -0.375 to 0.375
- grad_out: bfloat16 [98304, 256], P(('row', 'col')), may hold values from -6 to 6
- in_degree: int32 [98304], P(('row', 'col')), may hold values from 4 to 64
- out_degree: int32 [98304], P(('col', 'row')), may hold values from 4 to 64
- tile_edges: bfloat16 [8, 32, 192, 128, 128], P('row', 'col'), may hold values from 0 to 2, as said below
- tile_coords: int32 [8, 32, 192, 2], P('row', 'col'), may hold values from 0 to 95, as said below
- tile_count: int32 [8, 32], P('row', 'col'), may hold values from 48 to 192, as said below
Outputs:
- hidden: bfloat16 [98304, 256], P(('row', 'col'))
- grad_embedding: float32 [98304, 256], P(('col', 'row'))
- grad_weight: float32 [256, 256], replicated
The draws below stay inside these ranges and needn't reach their ends.
Inputs may be any that keep to these rules, and one draw needn't show every extreme that they name: `tile_coords`: slots of one block name distinct tiles; entry 0 is a tile row below 96, entry 1 a tile column below 24. The live slots of a block are its first tile_count slots; some block has all 192 slots live. `tile_edges`: each entry is zero or a positive edge weight.
All inputs are finite; a program needn't handle non-finite values.
Results may differ from the reference program's by a relative error of at most 0.033.
Values may be sent and summed in bfloat16 or wider, within the bound.
No kernel may reach another device: no remote copies, remote signals or barrier semaphores. Data moves between devices by JAX's collectives and lax.ppermute only.
A program may use at most 128 MiB of HBM per device.

```python
import jax
import jax.numpy as jnp
from jax import lax

F = 256
TILE = 128
ROWS_DEV = 384
NODES = 98304
TILE_ROWS = 96
TILE_COLS = 24
TILES_DEV = 192
N_ROW = 8
N_COL = 32
DEVICES = 256


def draw_tile_edges(key, part):
    first, second = jax.random.split(jax.random.fold_in(key, 11))
    shape = (N_ROW, N_COL, TILES_DEV, TILE, TILE)
    present = jax.random.uniform(first, shape, jnp.float32) < 0.02
    values = jax.random.uniform(second, shape, jnp.float32, 0.5, 1.5)
    return jnp.where(present, values, 0.0).astype(jnp.bfloat16)


def pick_tiles(single_key):
    return jax.random.permutation(single_key, TILE_ROWS * TILE_COLS)[:TILES_DEV]


def draw_tile_coords(key, part):
    keys = jax.random.split(jax.random.fold_in(key, 7), N_ROW * N_COL)
    picks = jax.vmap(pick_tiles)(keys).astype(jnp.int32)
    tile_row = picks // TILE_COLS
    tile_col = picks % TILE_COLS
    stacked = jnp.stack([tile_row, tile_col], axis=-1)
    return stacked.reshape(N_ROW, N_COL, TILES_DEV, 2).astype(jnp.int32)


def draw_tile_count(key, part):
    first, second = jax.random.split(jax.random.fold_in(key, 3))
    lowest = max(1, TILES_DEV // 4)
    counts = jax.random.randint(first, (N_ROW * N_COL,), lowest, TILES_DEV + 1)
    fullest = jax.random.randint(second, (), 0, N_ROW * N_COL)
    counts = jnp.where(jnp.arange(N_ROW * N_COL) == fullest, TILES_DEV, counts)
    return counts.reshape(N_ROW, N_COL).astype(jnp.int32)


def place_ends(array, own_key, low, largest):
    longest = array.shape.index(max(array.shape))
    spots = []
    for shift in (0, 1):
        where = [jax.random.randint(jax.random.fold_in(own_key, axis), (), 0, length) for axis, length in enumerate(array.shape)]
        where[longest] = (where[longest] + shift) % array.shape[longest]
        spots.append(tuple(where))
    return array.at[spots[0]].set(low).at[spots[1]].set(largest)


def block_scale(stream_key, shape, cuts, low, top_value):
    def one(position, shards_of):
        steps = jax.random.uniform(jax.random.fold_in(jax.random.fold_in(stream_key, 6), position), (shards_of,), jnp.float32, low / len(cuts), top_value / len(cuts))
        return jnp.repeat(jnp.exp(steps), shape[position] // shards_of).reshape((-1,) + (1,) * (len(shape) - position - 1))

    gain = one(*cuts[0])
    for cut in cuts[1:]:
        gain = gain * one(*cut)
    return gain


def gaussian(own_key, shape, spread, limit, shards=(), kind=jnp.bfloat16):
    values = spread * jax.random.normal(own_key, shape, jnp.float32)
    if shards:
        values = values * block_scale(own_key, shape, shards, -0.22, 0.18)
    return jnp.clip(values, -limit, limit).astype(kind)


def setup_inputs(seed: int = 0) -> dict:
    seeds = jax.random.split(jax.random.key(seed), 9)
    embedding = gaussian(seeds[0], (NODES, F), 1.0, 6.0, ((0, 256),))
    weight = gaussian(seeds[1], (F, F), F ** -0.5, 0.375)
    grad_out = gaussian(seeds[2], (NODES, F), 1.0, 6.0, ((0, 256),))
    in_degree = place_ends(jax.random.randint(seeds[3], (NODES,), 4, 65), jax.random.fold_in(seeds[3], 1), 4, 64).astype(jnp.int32)
    out_degree = place_ends(jax.random.randint(seeds[4], (NODES,), 4, 65), jax.random.fold_in(seeds[4], 1), 4, 64).astype(jnp.int32)
    tile_edges = draw_tile_edges(jax.random.fold_in(seeds[8], 71), 0)
    tile_coords = draw_tile_coords(jax.random.fold_in(seeds[8], 71), 0)
    tile_count = draw_tile_count(jax.random.fold_in(seeds[8], 71), 0)
    return dict(embedding=embedding, weight=weight, grad_out=grad_out, in_degree=in_degree, out_degree=out_degree, tile_edges=tile_edges, tile_coords=tile_coords, tile_count=tile_count)


decay_rate = 0.01

def block_pass(total, tile_edges, tile_coords, tile_count, lookup, flipped):
    width = lookup.shape[1]
    block_rows = ROWS_DEV * N_COL
    block_cols = ROWS_DEV * N_ROW
    flat_edges = tile_edges.reshape(DEVICES, TILES_DEV, TILE, TILE)
    flat_coords = tile_coords.reshape(DEVICES, TILES_DEV, 2)
    flat_count = tile_count.reshape(DEVICES)

    def advance(running, number):
        row_id = (number // N_COL).astype(jnp.int32)
        col_id = (number % N_COL).astype(jnp.int32)
        tile_set = flat_edges[number].astype(jnp.float32)
        coords = flat_coords[number]
        alive = (jnp.arange(TILES_DEV, dtype=jnp.int32) < flat_count[number]).astype(jnp.float32)
        if flipped:
            source = lax.dynamic_slice_in_dim(lookup, (row_id * block_rows).astype(jnp.int32), block_rows, 0)
            source = source.reshape(TILE_ROWS, TILE, width)
            picked = source[coords[:, 0]].astype(jnp.float32)
            products = jnp.einsum('tij,tif->tjf', tile_set, picked) * alive[:, None, None]
            partial_value = jnp.zeros((TILE_COLS, TILE, width), jnp.float32).at[coords[:, 1]].add(products)
            partial_value = partial_value.reshape(block_cols, width).astype(jnp.bfloat16)
            partial_value = lax.optimization_barrier(partial_value).astype(jnp.float32)
            offset = (col_id * block_cols).astype(jnp.int32)
            current = lax.dynamic_slice_in_dim(running, offset, block_cols, 0)
            running = lax.dynamic_update_slice_in_dim(running, current + partial_value, offset, 0)
        else:
            source = lax.dynamic_slice_in_dim(lookup, (col_id * block_cols).astype(jnp.int32), block_cols, 0)
            source = source.reshape(TILE_COLS, TILE, width)
            picked = source[coords[:, 1]].astype(jnp.float32)
            products = jnp.einsum('tij,tjf->tif', tile_set, picked) * alive[:, None, None]
            partial_value = jnp.zeros((TILE_ROWS, TILE, width), jnp.float32).at[coords[:, 0]].add(products)
            partial_value = partial_value.reshape(block_rows, width).astype(jnp.bfloat16)
            partial_value = lax.optimization_barrier(partial_value).astype(jnp.float32)
            offset = (row_id * block_rows).astype(jnp.int32)
            current = lax.dynamic_slice_in_dim(running, offset, block_rows, 0)
            running = lax.dynamic_update_slice_in_dim(running, current + partial_value, offset, 0)
        return (running, None)
    result, _ = lax.scan(advance, total, jnp.arange(DEVICES, dtype=jnp.int32))
    return result

def reference(embedding, weight, grad_out, in_degree, out_degree, tile_edges, tile_coords, tile_count):
    width = embedding.shape[1]
    scale_out = lax.rsqrt(out_degree.astype(jnp.float32))
    scale_in = lax.rsqrt(in_degree.astype(jnp.float32))
    scaled = (scale_out[:, None] * embedding.astype(jnp.float32)).astype(jnp.bfloat16)
    summed = block_pass(jnp.zeros((NODES, width), jnp.float32), tile_edges, tile_coords, tile_count, scaled, False)
    aggregate = (scale_in[:, None] * summed).astype(jnp.bfloat16)
    preact = jnp.dot(aggregate, weight, preferred_element_type=jnp.float32)
    gates = jax.nn.sigmoid(preact)
    hidden = (preact * gates).astype(jnp.bfloat16)
    delta = (grad_out.astype(jnp.float32) * gates * (1.0 + preact * (1.0 - gates))).astype(jnp.bfloat16)
    grad_weight = jnp.dot(aggregate.T, delta, preferred_element_type=jnp.float32) / jnp.sqrt(jnp.float32(NODES))
    upstream = (scale_in[:, None] * jnp.dot(delta, weight.T, preferred_element_type=jnp.float32)).astype(jnp.bfloat16)
    source_total = block_pass(jnp.zeros((NODES, width), jnp.float32), tile_edges, tile_coords, tile_count, upstream, True)
    decay = decay_rate * jnp.sqrt(out_degree.astype(jnp.float32))
    grad_embedding = scale_out[:, None] * source_total + decay[:, None] * embedding.astype(jnp.float32)
    return (hidden, grad_embedding, grad_weight)
```

```python
import functools
import math

import jax
import jax.numpy as jnp
from jax import lax
from jax.experimental import pallas as pl
from jax.experimental.pallas import tpu as pltpu
from jax.sharding import PartitionSpec as P

decay_rate = 0.01
f32 = jnp.float32
bf16 = jnp.bfloat16

chunks = ((0, 1, 2),)
unroll = 16
padded = 256

x_bit, z_bit, y_bit = 1, 3, 1


def exchange(value, axis, mask):
    size = lax.axis_size(axis)
    return lax.ppermute(value, axis, [(i, i ^ mask) for i in range(size)])


def group_kernel(table, tiles, source, *rest, group, flipped, carried):
    previous = rest[0] if carried else None
    out = rest[-1]

    def clear(i, _):
        if carried:
            out[i] = previous[i].astype(out.dtype)
        else:
            out[i] = jnp.zeros(out.shape[1:], out.dtype)
        return 0

    lax.fori_loop(0, out.shape[0], clear, 0)
    slots = tiles.shape[0]
    start = table[slots + group]
    stop = table[slots + group + 1]
    dims = (((0,), (0,)), ((), ())) if flipped else (((1,), (0,)), ((), ()))

    def advance(number, total):
        for step in range(unroll):
            index = start + number * unroll + step
            real = index < stop
            entry = table[jnp.minimum(index, stop - 1)]
            slot = entry & 255
            place = (entry >> 8) & 255
            origin = (entry >> 16) & 255
            fresh = jnp.logical_and(real, (entry >> 24) == 1)
            product = lax.dot_general(
                tiles[slot], source[origin], dims, preferred_element_type=f32
            )
            product = product * real.astype(f32)
            if carried:
                total = jnp.where(fresh, previous[place], total) + product
            else:
                total = total * (1.0 - fresh.astype(f32)) + product
            out[place] = total.astype(out.dtype)
        return total

    steps = (stop - start + unroll - 1) // unroll
    lax.fori_loop(0, steps, advance, jnp.zeros(out.shape[1:], f32))


def group_products(table, tiles, source, count, group, flipped, previous=None, dtype=bf16):
    slots, edge, _ = tiles.shape
    width = source.shape[2]
    operands = (table, tiles, source) + (() if previous is None else (previous,))
    whole = pl.BlockSpec(memory_space=pltpu.VMEM)
    return pl.pallas_call(
        functools.partial(
            group_kernel, group=group, flipped=flipped, carried=previous is not None
        ),
        out_shape=jax.ShapeDtypeStruct((count, edge, width), dtype),
        in_specs=[pl.BlockSpec(memory_space=pltpu.SMEM)] + [whole] * (len(operands) - 1),
        out_specs=whole,
        compiler_params=pltpu.CompilerParams(vmem_limit_bytes=40 << 20),
        cost_estimate=pl.CostEstimate(
            flops=2 * count * edge * edge * width,
            bytes_accessed=count * edge * width * 2,
            transcendentals=0,
        ),
        name=("backward" if flipped else "forward") + str(group),
    )(*operands)


def slot_table(key, place, origin, groups):
    slots = key.shape[0]
    number = jnp.arange(slots, dtype=jnp.int32)
    earlier = number[None, :] < number[:, None]
    same = key[None, :] == key[:, None]
    ahead = jnp.logical_or(key[None, :] < key[:, None], jnp.logical_and(same, earlier))
    rank = jnp.sum(ahead.astype(jnp.int32), axis=1)
    repeats = jnp.sum(jnp.logical_and(same, earlier).astype(jnp.int32), axis=1)
    fresh = (repeats == 0).astype(jnp.int32)
    packed = number | (place << 8) | (origin << 16) | (fresh << 24)
    hit = rank[None, :] == number[:, None]
    ordered = jnp.sum(jnp.where(hit, packed[None, :], 0), axis=1)
    limits = jnp.arange(padded - slots, dtype=jnp.int32) * 128
    bounds = jnp.sum((key[None, :] < limits[:, None]).astype(jnp.int32), axis=1)
    live = jnp.sum((key < groups * 128).astype(jnp.int32))
    return jnp.concatenate([ordered, jnp.minimum(bounds, live)])


def slot_tables(coords, live_count, own_col, own_row, per_owner):
    tile_row = coords[:, 0]
    tile_col = coords[:, 1]
    alive = jnp.arange(coords.shape[0], dtype=jnp.int32) < live_count
    apart = (tile_row // per_owner) ^ own_col
    part = tile_row % per_owner
    core = apart & 1
    x = (apart >> x_bit) & 3
    z = (apart >> z_bit) & 3
    low = jnp.where(x == 0, 8, jnp.where(x == 1, 0, jnp.where(x == 2, 2, 10)))
    high = jnp.where(x == 0, 12, jnp.where(x == 1, 14, jnp.where(x == 2, 4, 6)))
    block = jnp.where(z < 2, low, high) + (z & 1)
    later = block // 8
    chunk = jnp.zeros_like(part)
    inner = jnp.zeros_like(part)
    breadth = jnp.zeros_like(part)
    for k, members in enumerate(chunks):
        for i, member in enumerate(members):
            chunk = jnp.where(part == member, k, chunk)
            inner = jnp.where(part == member, i, inner)
            breadth = jnp.where(part == member, len(members), breadth)
    row_apart = (tile_col // per_owner) ^ own_row
    source_place = ((row_apart & 1) * 4 + (row_apart >> y_bit)) * per_owner + tile_col % per_owner
    forward_place = (block & 7) * breadth + inner
    forward_key = (chunk * 4 + later * 2 + 1 - core) * 128 + forward_place
    backward_origin = (core * 16 + x * 4 + z) * breadth + inner
    backward_key = chunk * 128 + source_place
    dead = 1 << 20

    def table(key, place, origin, groups):
        return slot_table(
            jnp.where(alive, key, dead),
            jnp.where(alive, place, 0),
            jnp.where(alive, origin, 0),
            groups,
        )

    forward = table(forward_key, forward_place, source_place, 4 * len(chunks))
    backward = table(backward_key, source_place, backward_origin, len(chunks))
    return forward, backward


def ring_gather(block, axis, bit):
    near, far = 1 << bit, 3 << bit
    half = block.shape[0] // 2
    first = exchange(block, axis, near)
    third = exchange(block, axis, far)
    second_low = exchange(first[:half], axis, far)
    second_high = exchange(third[half:], axis, near)
    return [block, first, second_low, second_high, third]


def wide(value):
    return value.astype(f32)


def reduce_row(terms):
    near, far = 1 << y_bit, 3 << y_bit
    low, high = terms[0], terms[1]
    low_in = exchange(low[1:3], "row", near)
    high_in = exchange(high[2:4], "row", far)
    low_next = exchange((wide(low[3]) + wide(low_in[1])).astype(bf16), "row", far)
    high_next = exchange((wide(high[1]) + wide(high_in[0])).astype(bf16), "row", near)
    leaving = (wide(high[0]) + wide(high_in[1]) + wide(high_next)).astype(bf16)
    arrived = exchange(leaving, "row", 1)
    return wide(low[0]) + wide(low_in[0]) + wide(low_next) + wide(arrived)


def reduce_weight(term, own_col):
    rows = term.shape[0]
    half, eighth = rows // 2, rows // 8
    core = own_col & 1
    x = (own_col >> x_bit) & 3
    mine = lax.dynamic_slice_in_dim(term, core * half, half, 0)
    other = lax.dynamic_slice_in_dim(term, (1 - core) * half, half, 0)
    mine = mine + exchange(other, "col", 1)
    share = lax.dynamic_slice_in_dim(mine, x * eighth, eighth, 0)
    for distance in (1, 2, 3):
        piece = lax.dynamic_slice_in_dim(mine, (x ^ distance) * eighth, eighth, 0)
        share = share + exchange(piece, "col", distance << x_bit)
    for axis, mask in (("col", 1 << z_bit), ("col", 2 << z_bit), ("row", 1 << y_bit), ("row", 3 << y_bit), ("row", 1)):
        share = share + exchange(share, axis, mask)
    total = jnp.zeros((half, term.shape[1]), f32)
    total = lax.dynamic_update_slice_in_dim(total, share, x * eighth, 0)
    for distance in (1, 2, 3):
        piece = exchange(share, "col", distance << x_bit)
        total = lax.dynamic_update_slice_in_dim(total, piece, (x ^ distance) * eighth, 0)
    other = exchange(total, "col", 1)
    lower = jnp.where(core == 0, total, other)
    upper = jnp.where(core == 0, other, total)
    return jnp.concatenate([lower, upper], axis=0)


def per_device(
    embedding, weight, grad_out, in_degree, out_degree, tile_edges, tile_coords, tile_count
):
    tiles = tile_edges[0, 0]
    n_row = lax.axis_size("row")
    n_col = lax.axis_size("col")
    own_row = lax.axis_index("row").astype(jnp.int32)
    own_col = lax.axis_index("col").astype(jnp.int32)
    own_rows, width = embedding.shape
    edge = tiles.shape[1]
    per_owner = own_rows // edge
    total_nodes = own_rows * n_row * n_col
    forward_table, backward_table = slot_tables(
        tile_coords[0, 0], tile_count[0, 0], own_col, own_row, per_owner
    )

    scale_out = lax.rsqrt(out_degree.astype(f32))
    scale_in = lax.rsqrt(in_degree.astype(f32))
    scaled = (scale_out[:, None] * wide(embedding)).astype(bf16)
    gathered = ring_gather(scaled, "row", y_bit)
    gathered += ring_gather(exchange(scaled, "row", 1), "row", y_bit)
    source = jnp.concatenate(gathered, axis=0).reshape(n_row * per_owner, edge, width)

    near, far = 1 << x_bit, 3 << x_bit
    upstream_parts = []
    hidden_parts = []
    local_weight = jnp.zeros((width, width), f32)
    for k, members in enumerate(chunks):
        count = 8 * len(members)
        rows = len(members) * edge

        def products(group):
            return group_products(forward_table, tiles, source, count, 4 * k + group, False)

        def blocks(value):
            return value.reshape(8, rows, width)

        leaving = products(0)
        early_in = blocks(exchange(leaving, "col", 1))
        early = blocks(products(1))
        leaving = products(2)
        late_in = blocks(exchange(leaving, "col", 1))
        late = blocks(products(3))

        def first_sum(low, high):
            return (wide(early[low:high]) + wide(early_in[low:high])).astype(bf16)

        def late_sum(low, high):
            return wide(late[low:high]) + wide(late_in[low:high])

        low_in = exchange(first_sum(0, 4), "col", near)
        high_in = exchange(first_sum(4, 8), "col", far)
        low_next = exchange((late_sum(2, 4) + wide(low_in[2:4])).astype(bf16), "col", far)
        high_next = exchange((late_sum(6, 8) + wide(high_in[0:2])).astype(bf16), "col", near)
        low = late_sum(0, 2) + wide(low_in[0:2]) + wide(low_next)
        high = late_sum(4, 6) + wide(high_in[2:4]) + wide(high_next)
        summed = low[0]
        for distance, leaving in ((1, low[1]), (2, high[0]), (3, high[1])):
            summed = summed + wide(
                exchange(leaving.astype(bf16), "col", distance << z_bit)
            )

        def own(value):
            return jnp.concatenate([value[m * edge : (m + 1) * edge] for m in members], axis=0)

        chunk_scale = own(scale_in)
        aggregate = (chunk_scale[:, None] * summed).astype(bf16)
        preact = jnp.dot(aggregate, weight, preferred_element_type=f32)
        gates = jax.nn.sigmoid(preact)
        hidden_parts.append((preact * gates).astype(bf16))
        delta = (wide(own(grad_out)) * gates * (1.0 + preact * (1.0 - gates))).astype(bf16)
        local_weight = local_weight + lax.dot_general(
            aggregate, delta, (((0,), (0,)), ((), ())), preferred_element_type=f32
        )
        projected = lax.dot_general(
            delta, weight, (((1,), (1,)), ((), ())), preferred_element_type=f32
        )
        upstream = (chunk_scale[:, None] * projected).astype(bf16)
        stack = [upstream] + [
            exchange(upstream, "col", distance << z_bit) for distance in (1, 2, 3)
        ]
        upstream_parts.append(jnp.concatenate(stack, axis=0))

    hidden = jnp.concatenate(hidden_parts, axis=0)
    grad_weight = reduce_weight(local_weight, own_col) / math.sqrt(total_nodes)

    terms = None
    for k, members in enumerate(chunks):
        pieces = ring_gather(upstream_parts[k], "col", x_bit)
        pieces += [exchange(piece, "col", 1) for piece in pieces]
        block = jnp.concatenate(pieces, axis=0).reshape(n_col * len(members), edge, width)
        last = k == len(chunks) - 1
        terms = group_products(
            backward_table,
            tiles,
            block,
            n_row * per_owner,
            k,
            True,
            terms,
            bf16 if last else f32,
        )
    source_total = reduce_row(terms.reshape(2, 4, own_rows, width))
    decay = decay_rate * jnp.sqrt(out_degree.astype(f32))
    grad_embedding = scale_out[:, None] * source_total + decay[:, None] * wide(embedding)
    return (hidden, grad_embedding, grad_weight)


def solution(mesh):
    in_specs = (
        P(("col", "row"), None),
        P(),
        P(("row", "col"), None),
        P(("row", "col")),
        P(("col", "row")),
        P("row", "col", None, None, None),
        P("row", "col", None, None),
        P("row", "col"),
    )
    out_specs = (P(("row", "col"), None), P(("col", "row"), None), P())
    return jax.shard_map(
        per_device, mesh=mesh, in_specs=in_specs, out_specs=out_specs, check_vma=False
    )
```

```python
import functools
import math

import jax
import jax.numpy as jnp
from jax import lax
from jax.experimental import pallas as pl
from jax.experimental.pallas import tpu as pltpu
from jax.sharding import PartitionSpec as P

decay_rate = 0.01
f32 = jnp.float32
bf16 = jnp.bfloat16

chunks = ((0,), (1, 2))
unroll = 8
depth = 4
padded = 256

x_bit, z_bit, y_bit = 1, 3, 1


def exchange(value, axis, mask):
    size = lax.axis_size(axis)
    return lax.ppermute(value, axis, [(i, i ^ mask) for i in range(size)])


def after(value, earlier):
    return lax.optimization_barrier((value, earlier))[0]


def group_kernel(table, tiles, *rest, spans, group, flipped, carried):
    pieces = rest[: len(spans)]
    previous = rest[len(spans)] if carried else None
    out, source, ring, piece_sems, ring_sems = rest[-5:]
    slots, edge, _ = tiles.shape
    start = table[slots + group]
    stop = table[slots + group + 1]
    steps = (stop - start + unroll - 1) // unroll
    final = jnp.maximum(stop - 1, 0)

    def fetches(number):
        place = lax.rem(number, depth)
        found = []
        for step in range(unroll):
            entry = table[jnp.minimum(start + number * unroll + step, final)]
            found.append(
                pltpu.make_async_copy(
                    tiles.at[entry & 255], ring.at[place, step], ring_sems.at[place, step]
                )
            )
        return found

    def begin(number, _):
        for fetch in fetches(number):
            fetch.start()
        return 0

    def finish(number, _):
        for fetch in fetches(number):
            fetch.wait()
        return 0

    lax.fori_loop(0, depth - 1, begin, 0)
    row = 0
    copies = []
    for number, (piece, span) in enumerate(zip(pieces, spans)):
        copies.append(
            pltpu.make_async_copy(
                piece.at[:span], source.at[row : row + span], piece_sems.at[number]
            )
        )
        copies[-1].start()
        row += span

    def clear(i, _):
        if carried:
            out[i] = previous[i].astype(out.dtype)
        else:
            out[i] = jnp.zeros(out.shape[1:], out.dtype)
        return 0

    lax.fori_loop(0, out.shape[0], clear, 0)
    for copy in copies:
        copy.wait()
    dims = (((0,), (0,)), ((), ())) if flipped else (((1,), (0,)), ((), ()))

    def advance(number, total):
        begin(number + depth - 1, 0)
        finish(number, 0)
        held = lax.rem(number, depth)
        for step in range(unroll):
            index = start + number * unroll + step
            real = index < stop
            entry = table[jnp.minimum(index, final)]
            place = (entry >> 8) & 255
            origin = pl.multiple_of(((entry >> 16) & 255) * edge, edge)
            fresh = jnp.logical_and(real, (entry >> 24) == 1)
            product = lax.dot_general(
                ring[held, step], source[pl.ds(origin, edge)], dims, preferred_element_type=f32
            )
            product = product * real.astype(f32)
            if carried:
                total = jnp.where(fresh, previous[place], total) + product
            else:
                total = total * (1.0 - fresh.astype(f32)) + product
            out[place] = total.astype(out.dtype)
        return total

    lax.fori_loop(0, steps, advance, jnp.zeros(out.shape[1:], f32))
    lax.fori_loop(steps, steps + depth - 1, finish, 0)


def group_products(table, tiles, pieces, count, group, flipped, previous=None, dtype=bf16):
    slots, edge, _ = tiles.shape
    arrays = [array for array, _ in pieces]
    spans = [span for _, span in pieces]
    width = arrays[0].shape[1]
    operands = [table, tiles] + arrays + ([] if previous is None else [previous])
    anywhere = pl.BlockSpec(memory_space=pl.ANY)
    whole = pl.BlockSpec(memory_space=pltpu.VMEM)
    return pl.pallas_call(
        functools.partial(
            group_kernel,
            spans=spans,
            group=group,
            flipped=flipped,
            carried=previous is not None,
        ),
        out_shape=jax.ShapeDtypeStruct((count, edge, width), dtype),
        in_specs=[pl.BlockSpec(memory_space=pltpu.SMEM)]
        + [anywhere] * (1 + len(arrays))
        + [whole] * (previous is not None),
        out_specs=whole,
        scratch_shapes=[
            pltpu.VMEM((sum(spans), width), bf16),
            pltpu.VMEM((depth, unroll, edge, edge), bf16),
            pltpu.SemaphoreType.DMA((len(arrays),)),
            pltpu.SemaphoreType.DMA((depth, unroll)),
        ],
        compiler_params=pltpu.CompilerParams(vmem_limit_bytes=24 << 20),
        cost_estimate=pl.CostEstimate(
            flops=2 * slots * edge * edge * width // 4,
            bytes_accessed=count * edge * width * 4,
            transcendentals=0,
        ),
        name=("backward" if flipped else "forward") + str(group),
    )(*operands)


def slot_table(key, place, origin, groups):
    slots = key.shape[0]
    number = jnp.arange(slots, dtype=jnp.int32)
    earlier = number[None, :] < number[:, None]
    same = key[None, :] == key[:, None]
    ahead = jnp.logical_or(key[None, :] < key[:, None], jnp.logical_and(same, earlier))
    rank = jnp.sum(ahead.astype(jnp.int32), axis=1)
    repeats = jnp.sum(jnp.logical_and(same, earlier).astype(jnp.int32), axis=1)
    fresh = (repeats == 0).astype(jnp.int32)
    packed = number | (place << 8) | (origin << 16) | (fresh << 24)
    hit = rank[None, :] == number[:, None]
    ordered = jnp.sum(jnp.where(hit, packed[None, :], 0), axis=1)
    limits = jnp.arange(padded - slots, dtype=jnp.int32) * 128
    bounds = jnp.sum((key[None, :] < limits[:, None]).astype(jnp.int32), axis=1)
    live = jnp.sum((key < groups * 128).astype(jnp.int32))
    return jnp.concatenate([ordered, jnp.minimum(bounds, live)])


def slot_tables(coords, live_count, own_col, own_row, per_owner):
    tile_row = coords[:, 0]
    tile_col = coords[:, 1]
    alive = jnp.arange(coords.shape[0], dtype=jnp.int32) < live_count
    apart = (tile_row // per_owner) ^ own_col
    part = tile_row % per_owner
    core = apart & 1
    x = (apart >> x_bit) & 3
    z = (apart >> z_bit) & 3
    block = (z >> 1) * 8 + x * 2 + (z & 1)
    chunk = jnp.zeros_like(part)
    inner = jnp.zeros_like(part)
    breadth = jnp.zeros_like(part)
    for k, members in enumerate(chunks):
        for i, member in enumerate(members):
            chunk = jnp.where(part == member, k, chunk)
            inner = jnp.where(part == member, i, inner)
            breadth = jnp.where(part == member, len(members), breadth)
    row_apart = (tile_col // per_owner) ^ own_row
    source_place = ((row_apart & 1) * 4 + (row_apart >> y_bit)) * per_owner + tile_col % per_owner
    forward_place = block * breadth + inner
    forward_key = (chunk * 2 + 1 - core) * 128 + forward_place
    backward_origin = (core * 16 + x * 4 + z) * breadth + inner
    backward_key = chunk * 128 + source_place
    dead = 1 << 20

    def table(key, place, origin, groups):
        return slot_table(
            jnp.where(alive, key, dead),
            jnp.where(alive, place, 0),
            jnp.where(alive, origin, 0),
            groups,
        )

    forward = table(forward_key, forward_place, source_place, 2 * len(chunks))
    backward = table(backward_key, source_place, backward_origin, len(chunks))
    return forward, backward


def ring_gather(block, axis, bit, half):
    near, far = 1 << bit, 3 << bit
    first = exchange(block, axis, near)
    third = exchange(block, axis, far)
    second_low = exchange(first[:half], axis, far)
    second_high = exchange(third[half:], axis, near)
    return [block, first, second_low, second_high, third]


def wide(value):
    return value.astype(f32)


def reduce_row(terms):
    near, far = 1 << y_bit, 3 << y_bit
    low, high = terms[0], terms[1]
    low_in = exchange(low[1:3], "row", near)
    high_in = exchange(high[2:4], "row", far)
    low_next = exchange((wide(low[3]) + wide(low_in[1])).astype(bf16), "row", far)
    high_next = exchange((wide(high[1]) + wide(high_in[0])).astype(bf16), "row", near)
    leaving = (wide(high[0]) + wide(high_in[1]) + wide(high_next)).astype(bf16)
    arrived = exchange(leaving, "row", 1)
    return wide(low[0]) + wide(low_in[0]) + wide(low_next) + wide(arrived)


def per_device(
    embedding, weight, grad_out, in_degree, out_degree, tile_edges, tile_coords, tile_count
):
    tiles = tile_edges[0, 0]
    n_row = lax.axis_size("row")
    n_col = lax.axis_size("col")
    own_row = lax.axis_index("row").astype(jnp.int32)
    own_col = lax.axis_index("col").astype(jnp.int32)
    own_rows, width = embedding.shape
    edge = tiles.shape[1]
    per_owner = own_rows // edge
    total_nodes = own_rows * n_row * n_col

    scale_out = lax.rsqrt(out_degree.astype(f32))
    scale_in = lax.rsqrt(in_degree.astype(f32))
    scaled = (scale_out[:, None] * wide(embedding)).astype(bf16)
    across = exchange(scaled, "row", 1)
    source = ring_gather(scaled, "row", y_bit, own_rows // 2)
    source += ring_gather(across, "row", y_bit, own_rows // 2)
    source = [(piece, piece.shape[0]) for piece in source]
    forward_table, backward_table = slot_tables(
        tile_coords[0, 0], tile_count[0, 0], own_col, own_row, per_owner
    )

    near, far = 1 << x_bit, 3 << x_bit
    z = (own_col >> z_bit) & 3
    share_rows = width // 4
    number = range(len(chunks))
    heights = [len(members) * edge for members in chunks]

    def own(k, value):
        return jnp.concatenate([value[m * edge : (m + 1) * edge] for m in chunks[k]], axis=0)

    first_messages = []
    both = []
    for k in number:
        table = after(forward_table, first_messages[-1]) if k else forward_table
        count = 16 * len(chunks[k])
        shape = (2, 4, 2, heights[k], width)
        leaving = group_products(table, tiles, source, count, 2 * k, False)
        core_in = exchange(leaving, "col", 1).reshape(shape)
        kept = group_products(table, tiles, source, count, 2 * k + 1, False).reshape(shape)

        def sums(half, low, high, kept=kept, core_in=core_in):
            return wide(kept[half, low:high]) + wide(core_in[half, low:high])

        both.append(sums)
        first_messages.append((sums(0, 1, 3).astype(bf16), sums(1, 2, 4).astype(bf16)))
    reduced = []
    second_messages = None
    for k in number:
        messages = first_messages[k]
        if k:
            messages = after(messages, second_messages)
        low_in = exchange(messages[0], "col", near)
        high_in = exchange(messages[1], "col", far)
        second_messages = (
            (both[k](0, 3, 4)[0] + wide(low_in[1])).astype(bf16),
            (both[k](1, 1, 2)[0] + wide(high_in[0])).astype(bf16),
        )
        low_next = exchange(second_messages[0], "col", far)
        high_next = exchange(second_messages[1], "col", near)
        low = both[k](0, 0, 1)[0] + wide(low_in[0]) + wide(low_next)
        high = both[k](1, 0, 1)[0] + wide(high_in[1]) + wide(high_next)
        reduced.append((low[0], low[1].astype(bf16), high[0].astype(bf16), high[1].astype(bf16)))

    hidden_parts = []
    local_weight = jnp.zeros((width, width), f32)
    stacks = []
    upstream = None
    for k in number:
        rows = heights[k]
        last = k == len(chunks) - 1
        blocks = reduced[k]
        if k:
            blocks = after(blocks, upstream)
        summed = blocks[0]
        for distance in (1, 2, 3):
            summed = summed + wide(exchange(blocks[distance], "col", distance << z_bit))
        if k:
            summed = after(summed, stacks[-1])
        chunk_scale = own(k, scale_in)
        aggregate = (chunk_scale[:, None] * summed).astype(bf16)
        preact = jnp.dot(aggregate, weight, preferred_element_type=f32)
        gates = jax.nn.sigmoid(preact)
        hidden_parts.append((preact * gates).astype(bf16))
        delta = (wide(own(k, grad_out)) * gates * (1.0 + preact * (1.0 - gates))).astype(bf16)
        local_weight = local_weight + lax.dot_general(
            aggregate, delta, (((0,), (0,)), ((), ())), preferred_element_type=f32
        )
        projected = lax.dot_general(
            delta, weight, (((1,), (1,)), ((), ())), preferred_element_type=f32
        )
        upstream = (chunk_scale[:, None] * projected).astype(bf16)

        def weight_share(distance):
            return lax.dynamic_slice_in_dim(
                local_weight, (z ^ distance) * share_rows, share_rows, 0
            )

        stack = [upstream]
        if last:
            share = weight_share(0)
        for distance in (1, 2, 3):
            message = upstream
            if last:
                message = jnp.concatenate([upstream, weight_share(distance).astype(bf16)], axis=0)
            message = exchange(message, "col", distance << z_bit)
            stack.append(message[:rows])
            if last:
                share = share + wide(message[rows:])
        if last:
            stack.append(share.astype(bf16))
        stacks.append(jnp.concatenate(stack, axis=0))

    terms = None
    for k in number:
        rows = heights[k]
        last = k == len(chunks) - 1
        stack = stacks[k]
        if k:
            stack = after(stack, (second_low, second_high))
        first = exchange(stack, "col", near)
        third = exchange(stack, "col", far)
        if k:
            terms = products(k - 1)
            first, third = after((first, third), terms)
        low = first[: 2 * rows]
        if last:
            low = jnp.concatenate([low, first[4 * rows :]], axis=0)
        second_low = exchange(low, "col", far)
        second_high = exchange(third[2 * rows : 4 * rows], "col", near)
        if last:
            share = share + wide(first[4 * rows :]) + wide(third[4 * rows :])
            share = share + wide(second_low[2 * rows :])
        pieces = [
            (stack, 4 * rows),
            (first, 4 * rows),
            (second_low, 2 * rows),
            (second_high, 2 * rows),
            (third, 4 * rows),
        ]

        def products(k, last=last, pieces=pieces, terms=terms):
            arrived = [(exchange(piece[:span], "col", 1), span) for piece, span in pieces]
            return group_products(
                backward_table,
                tiles,
                pieces + arrived,
                n_row * per_owner,
                k,
                True,
                terms,
                bf16 if last else f32,
            )

    terms = products(len(chunks) - 1)
    source_total = reduce_row(terms.reshape(2, 4, own_rows, width))
    decay = decay_rate * jnp.sqrt(out_degree.astype(f32))
    grad_embedding = scale_out[:, None] * source_total + decay[:, None] * wide(embedding)

    for axis, mask in (("col", 1), ("row", 1 << y_bit), ("row", 3 << y_bit), ("row", 1)):
        share = share + exchange(share, axis, mask)
    grad_weight = jnp.zeros((width, width), f32)
    for distance in (0, 1, 2, 3):
        piece = exchange(share, "col", distance << z_bit) if distance else share
        grad_weight = lax.dynamic_update_slice_in_dim(
            grad_weight, piece, (z ^ distance) * share_rows, 0
        )
    grad_weight = grad_weight / math.sqrt(total_nodes)
    hidden = jnp.concatenate(hidden_parts, axis=0)

    return (hidden, grad_embedding, grad_weight)


def solution(mesh):
    in_specs = (
        P(("col", "row"), None),
        P(),
        P(("row", "col"), None),
        P(("row", "col")),
        P(("col", "row")),
        P("row", "col", None, None, None),
        P("row", "col", None, None),
        P("row", "col"),
    )
    out_specs = (P(("row", "col"), None), P(("col", "row"), None), P())
    return jax.shard_map(
        per_device, mesh=mesh, in_specs=in_specs, out_specs=out_specs, check_vma=False
    )
```

```python
import functools
import math

import jax
import jax.numpy as jnp
from jax import lax
from jax.experimental import pallas as pl
from jax.experimental.pallas import tpu as pltpu
from jax.sharding import PartitionSpec as P

decay_rate = 0.01
f32 = jnp.float32
bf16 = jnp.bfloat16

chunks = ((0,), (1, 2))
unroll = 8
padded = 256

x_bit, z_bit, y_bit = 1, 3, 1


def exchange(value, axis, mask):
    size = lax.axis_size(axis)
    return lax.ppermute(value, axis, [(i, i ^ mask) for i in range(size)])


def after(value, earlier):
    return lax.optimization_barrier((value, earlier))[0]


def group_kernel(table, tiles, *rest, spans, group, flipped, carried):
    pieces = rest[: len(spans)]
    previous = rest[len(spans)] if carried else None
    out, source = rest[-2:]
    slots, edge, _ = tiles.shape
    row = 0
    for piece, span in zip(pieces, spans):

        def move(i, _, piece=piece, row=row):
            source[pl.ds(row + i * 64, 64)] = piece[pl.ds(i * 64, 64)]
            return 0

        lax.fori_loop(0, span // 64, move, 0)
        row += span

    def clear(i, _):
        if carried:
            out[i] = previous[i].astype(out.dtype)
        else:
            out[i] = jnp.zeros(out.shape[1:], out.dtype)
        return 0

    lax.fori_loop(0, out.shape[0], clear, 0)
    start = table[0, slots + group]
    stop = table[0, slots + group + 1]
    dims = (((0,), (0,)), ((), ())) if flipped else (((1,), (0,)), ((), ()))

    def advance(number, total):
        for step in range(unroll):
            index = start + number * unroll + step
            real = index < stop
            entry = table[0, jnp.minimum(index, stop - 1)]
            slot = entry & 255
            place = (entry >> 8) & 255
            origin = pl.multiple_of(((entry >> 16) & 255) * edge, edge)
            fresh = jnp.logical_and(real, (entry >> 24) == 1)
            product = lax.dot_general(
                tiles[slot], source[pl.ds(origin, edge)], dims, preferred_element_type=f32
            )
            product = product * real.astype(f32)
            if carried:
                total = jnp.where(fresh, previous[place], total) + product
            else:
                total = total * (1.0 - fresh.astype(f32)) + product
            out[place] = total.astype(out.dtype)
        return total

    steps = (stop - start + unroll - 1) // unroll
    lax.fori_loop(0, steps, advance, jnp.zeros(out.shape[1:], f32))


def group_products(table, tiles, pieces, count, group, flipped, previous=None, dtype=bf16):
    slots, edge, _ = tiles.shape
    arrays = [array for array, _ in pieces]
    spans = [span for _, span in pieces]
    width = arrays[0].shape[1]
    operands = [table, tiles] + arrays + ([] if previous is None else [previous])
    whole = pl.BlockSpec(memory_space=pltpu.VMEM)
    return pl.pallas_call(
        functools.partial(
            group_kernel,
            spans=spans,
            group=group,
            flipped=flipped,
            carried=previous is not None,
        ),
        out_shape=jax.ShapeDtypeStruct((count, edge, width), dtype),
        in_specs=[pl.BlockSpec(memory_space=pltpu.SMEM)] + [whole] * (len(operands) - 1),
        out_specs=whole,
        scratch_shapes=[pltpu.VMEM((sum(spans), width), bf16)],
        compiler_params=pltpu.CompilerParams(vmem_limit_bytes=24 << 20),
        cost_estimate=pl.CostEstimate(
            flops=2 * slots * edge * edge * width // 4,
            bytes_accessed=count * edge * width * 4,
            transcendentals=0,
        ),
        name=("backward" if flipped else "forward") + str(group),
    )(*operands)


def order_kernel(coords, place_info, tiles, forward, backward, *, per_owner):
    del tiles
    slots = coords.shape[0]
    shape = (slots, padded)
    own_col = place_info[0]
    own_row = place_info[1]
    live_count = place_info[2]
    number = lax.broadcasted_iota(jnp.int32, (slots, 1), 0)
    alive = number < live_count
    tile_row = coords[:, 0:1]
    tile_col = coords[:, 1:2]
    owner_row = ((tile_row.astype(f32) + 0.5) * (1.0 / per_owner)).astype(jnp.int32)
    owner_col = ((tile_col.astype(f32) + 0.5) * (1.0 / per_owner)).astype(jnp.int32)
    apart = owner_row ^ own_col
    part = tile_row - owner_row * per_owner
    core = apart & 1
    x = (apart >> x_bit) & 3
    z = (apart >> z_bit) & 3
    block = (z >> 1) * 8 + x * 2 + (z & 1)
    chunk = jnp.zeros_like(part)
    inner = jnp.zeros_like(part)
    breadth = jnp.zeros_like(part)
    for k, members in enumerate(chunks):
        for i, member in enumerate(members):
            chunk = jnp.where(part == member, k, chunk)
            inner = jnp.where(part == member, i, inner)
            breadth = jnp.where(part == member, len(members), breadth)
    row_apart = owner_col ^ own_row
    source_place = ((row_apart & 1) * 4 + (row_apart >> y_bit)) * per_owner
    source_place = source_place + tile_col - owner_col * per_owner
    forward_place = block * breadth + inner
    forward_key = (chunk * 2 + 1 - core) * 128 + forward_place
    backward_origin = (core * 16 + x * 4 + z) * breadth + inner
    backward_key = chunk * 128 + source_place

    lane = lax.broadcasted_iota(jnp.int32, shape, 1)
    sub = lax.broadcasted_iota(jnp.int32, shape, 0)
    limit = ((lane[0:1] - slots) * 128).astype(f32)
    lane_number = lane[0:1].astype(f32)

    def table(key, place, origin, groups, out):
        key = jnp.where(alive, key, 1 << 20).astype(f32)
        place = jnp.where(alive, place, 0)
        origin = jnp.where(alive, origin, 0)
        across = jnp.sum(jnp.where(lane == sub, key, 0.0), axis=0, keepdims=True)
        same = jnp.logical_and(across == key, lane < sub)
        ahead = jnp.logical_and(jnp.logical_or(across < key, same), lane < slots)
        rank = jnp.sum(jnp.where(ahead, 1.0, 0.0), axis=1, keepdims=True)
        repeats = jnp.sum(jnp.where(same, 1.0, 0.0), axis=1, keepdims=True)
        fresh = (repeats == 0.0).astype(jnp.int32)
        low = (number | (place << 8)).astype(f32)
        high = (origin | (fresh << 8)).astype(f32)
        hit = rank == lane_number
        low = jnp.sum(jnp.where(hit, low, 0.0), axis=0, keepdims=True).astype(jnp.int32)
        high = jnp.sum(jnp.where(hit, high, 0.0), axis=0, keepdims=True).astype(jnp.int32)
        bound = jnp.minimum(limit, groups * 128.0)
        bounds = jnp.sum(jnp.where(key < bound, 1.0, 0.0), axis=0, keepdims=True)
        out[...] = jnp.where(lane[0:1] < slots, low | (high << 16), bounds.astype(jnp.int32))

    table(forward_key, forward_place, source_place, 2 * len(chunks), forward)
    table(backward_key, source_place, backward_origin, len(chunks), backward)


def slot_tables(coords, live_count, own_col, own_row, per_owner, tiles):
    place_info = jnp.stack([own_col, own_row, live_count])
    whole = pl.BlockSpec(memory_space=pltpu.VMEM)
    result = jax.ShapeDtypeStruct((1, padded), jnp.int32)
    return pl.pallas_call(
        functools.partial(order_kernel, per_owner=per_owner),
        out_shape=(result, result),
        in_specs=[whole, pl.BlockSpec(memory_space=pltpu.SMEM), whole],
        out_specs=(whole, whole),
        compiler_params=pltpu.CompilerParams(vmem_limit_bytes=8 << 20),
        name="order",
    )(coords, place_info, tiles)


def ring_gather(block, axis, bit, half, earlier=None):
    near, far = 1 << bit, 3 << bit
    first = exchange(block, axis, near)
    third = exchange(block, axis, far)
    if earlier is not None:
        first, third = after((first, third), earlier)
    second_low = exchange(first[:half], axis, far)
    second_high = exchange(third[half:], axis, near)
    return [block, first, second_low, second_high, third]


def wide(value):
    return value.astype(f32)


def reduce_row(terms, share):
    near, far = 1 << y_bit, 3 << y_bit
    rows, width = terms.shape[2:]
    low, high = terms[0], terms[1]

    def send(value, mask):
        message = jnp.concatenate([value.reshape(-1, width), share.astype(bf16)], axis=0)
        message = exchange(message, "row", mask)
        split = message.shape[0] - share.shape[0]
        return message[:split].reshape(value.shape), share + wide(message[split:])

    high_in = exchange(high[2:4], "row", far)
    low_in, share = send(low[1:3], near)
    high_next = exchange((wide(high[1]) + wide(high_in[0])).astype(bf16), "row", near)
    low_next, share = send((wide(low[3]) + wide(low_in[1])).astype(bf16), far)
    leaving = (wide(high[0]) + wide(high_in[1]) + wide(high_next)).astype(bf16)
    arrived = exchange(leaving, "row", 1)
    return wide(low[0]) + wide(low_in[0]) + wide(low_next) + wide(arrived), share


def per_device(
    embedding, weight, grad_out, in_degree, out_degree, tile_edges, tile_coords, tile_count
):
    tiles = tile_edges[0, 0]
    n_row = lax.axis_size("row")
    n_col = lax.axis_size("col")
    own_row = lax.axis_index("row").astype(jnp.int32)
    own_col = lax.axis_index("col").astype(jnp.int32)
    own_rows, width = embedding.shape
    edge = tiles.shape[1]
    per_owner = own_rows // edge
    total_nodes = own_rows * n_row * n_col

    scale_out = lax.rsqrt(out_degree.astype(f32))
    scale_in = lax.rsqrt(in_degree.astype(f32))
    scaled = (scale_out[:, None] * wide(embedding)).astype(bf16)
    forward_table, backward_table = slot_tables(
        tile_coords[0, 0], tile_count[0, 0], own_col, own_row, per_owner, tiles
    )
    source = ring_gather(scaled, "row", y_bit, own_rows // 2)
    across = exchange(scaled, "row", 1)
    source += ring_gather(across, "row", y_bit, own_rows // 2, forward_table)
    source = [(piece, piece.shape[0]) for piece in source]

    near, far = 1 << x_bit, 3 << x_bit
    z = (own_col >> z_bit) & 3
    share_rows = width // 4
    number = range(len(chunks))
    heights = [len(members) * edge for members in chunks]

    def own(k, value):
        return jnp.concatenate([value[m * edge : (m + 1) * edge] for m in chunks[k]], axis=0)

    first_messages = []
    both = []
    for k in number:
        table = after(forward_table, first_messages[-1]) if k else forward_table
        count = 16 * len(chunks[k])
        shape = (2, 4, 2, heights[k], width)
        leaving = group_products(table, tiles, source, count, 2 * k, False)
        core_in = exchange(leaving, "col", 1).reshape(shape)
        kept = group_products(table, tiles, source, count, 2 * k + 1, False).reshape(shape)

        def sums(half, low, high, kept=kept, core_in=core_in):
            return wide(kept[half, low:high]) + wide(core_in[half, low:high])

        both.append(sums)
        first_messages.append((sums(0, 1, 3).astype(bf16), sums(1, 2, 4).astype(bf16)))
    reduced = []
    second_messages = None
    for k in number:
        messages = first_messages[k]
        if k:
            messages = after(messages, second_messages)
        low_in = exchange(messages[0], "col", near)
        high_in = exchange(messages[1], "col", far)
        second_messages = (
            (both[k](0, 3, 4)[0] + wide(low_in[1])).astype(bf16),
            (both[k](1, 1, 2)[0] + wide(high_in[0])).astype(bf16),
        )
        low_next = exchange(second_messages[0], "col", far)
        high_next = exchange(second_messages[1], "col", near)
        low = both[k](0, 0, 1)[0] + wide(low_in[0]) + wide(low_next)
        high = both[k](1, 0, 1)[0] + wide(high_in[1]) + wide(high_next)
        reduced.append((low[0], low[1].astype(bf16), high[0].astype(bf16), high[1].astype(bf16)))

    hidden_parts = []
    local_weight = jnp.zeros((width, width), f32)
    stacks = []
    upstream = None
    for k in number:
        rows = heights[k]
        last = k == len(chunks) - 1
        blocks = reduced[k]
        if k:
            blocks = after(blocks, upstream)
        summed = blocks[0]
        for distance in (1, 2, 3):
            summed = summed + wide(exchange(blocks[distance], "col", distance << z_bit))
        if k:
            summed = after(summed, stacks[-1])
        chunk_scale = own(k, scale_in)
        aggregate = (chunk_scale[:, None] * summed).astype(bf16)
        preact = jnp.dot(aggregate, weight, preferred_element_type=f32)
        gates = jax.nn.sigmoid(preact)
        hidden_parts.append((preact * gates).astype(bf16))
        delta = (wide(own(k, grad_out)) * gates * (1.0 + preact * (1.0 - gates))).astype(bf16)
        local_weight = local_weight + lax.dot_general(
            aggregate, delta, (((0,), (0,)), ((), ())), preferred_element_type=f32
        )
        projected = lax.dot_general(
            delta, weight, (((1,), (1,)), ((), ())), preferred_element_type=f32
        )
        upstream = (chunk_scale[:, None] * projected).astype(bf16)

        def weight_share(distance):
            return lax.dynamic_slice_in_dim(
                local_weight, (z ^ distance) * share_rows, share_rows, 0
            )

        stack = [upstream]
        if last:
            share = weight_share(0)
        for distance in (1, 2, 3):
            message = upstream
            if last:
                message = jnp.concatenate([upstream, weight_share(distance).astype(bf16)], axis=0)
            message = exchange(message, "col", distance << z_bit)
            stack.append(message[:rows])
            if last:
                share = share + wide(message[rows:])
        if last:
            stack.append(share.astype(bf16))
        stacks.append(jnp.concatenate(stack, axis=0))

    terms = None
    for k in number:
        rows = heights[k]
        last = k == len(chunks) - 1
        stack = stacks[k]
        if k:
            stack = after(stack, (second_low, second_high))
        first = exchange(stack, "col", near)
        third = exchange(stack, "col", far)
        if k:
            terms = products(k - 1)
            first, third = after((first, third), terms)
        low = first[: 2 * rows]
        if last:
            low = jnp.concatenate([low, first[4 * rows :]], axis=0)
        second_low = exchange(low, "col", far)
        second_high = exchange(third[2 * rows : 4 * rows], "col", near)
        if last:
            share = share + wide(first[4 * rows :]) + wide(third[4 * rows :])
            share = share + wide(second_low[2 * rows :])
        pieces = [
            (stack, 4 * rows),
            (first, 4 * rows),
            (second_low, 2 * rows),
            (second_high, 2 * rows),
            (third, 4 * rows),
        ]

        def products(k, last=last, pieces=pieces, terms=terms):
            arrived = [(exchange(piece[:span], "col", 1), span) for piece, span in pieces]
            return group_products(
                backward_table,
                tiles,
                pieces + arrived,
                n_row * per_owner,
                k,
                True,
                terms,
                bf16 if last else f32,
            )

    for axis, mask in (("col", 1), ("row", 1)):
        share = share + exchange(share, axis, mask)
    terms = products(len(chunks) - 1)
    source_total, share = reduce_row(terms.reshape(2, 4, own_rows, width), share)
    grad_weight = jnp.zeros((width, width), f32)
    for distance in (0, 1, 2, 3):
        piece = exchange(share, "col", distance << z_bit) if distance else share
        grad_weight = lax.dynamic_update_slice_in_dim(
            grad_weight, piece, (z ^ distance) * share_rows, 0
        )
    grad_weight = grad_weight / math.sqrt(total_nodes)
    decay = decay_rate * jnp.sqrt(out_degree.astype(f32))
    grad_embedding = scale_out[:, None] * source_total + decay[:, None] * wide(embedding)

    hidden = jnp.concatenate(hidden_parts, axis=0)
    return (hidden, grad_embedding, grad_weight)


def solution(mesh):
    in_specs = (
        P(("col", "row"), None),
        P(),
        P(("row", "col"), None),
        P(("row", "col")),
        P(("col", "row")),
        P("row", "col", None, None, None),
        P("row", "col", None, None),
        P("row", "col"),
    )
    out_specs = (P(("row", "col"), None), P(("col", "row"), None), P())
    return jax.shard_map(
        per_device, mesh=mesh, in_specs=in_specs, out_specs=out_specs, check_vma=False
    )
```

```python
import functools
import math

import jax
import jax.numpy as jnp
from jax import lax
from jax.experimental import pallas as pl
from jax.experimental.pallas import tpu as pltpu
from jax.sharding import PartitionSpec as P

decay_rate = 0.01
f32 = jnp.float32
bf16 = jnp.bfloat16

chunks = ((0,), (1, 2))
unroll = 8
padded = 256

x_bit, z_bit, y_bit = 1, 3, 1


def exchange(value, axis, mask):
    size = lax.axis_size(axis)
    return lax.ppermute(value, axis, [(i, i ^ mask) for i in range(size)])


def after(value, earlier):
    return lax.optimization_barrier((value, earlier))[0]


def group_kernel(table, tiles, *rest, spans, group, flipped, carried):
    pieces = rest[: len(spans)]
    previous = rest[len(spans)] if carried else None
    out, source = rest[-2:]
    slots, edge, _ = tiles.shape
    row = 0
    for piece, (first, span) in zip(pieces, spans):

        def move(i, _, piece=piece, row=row, first=first):
            source[pl.ds(row + i * 64, 64)] = piece[pl.ds(first + i * 64, 64)]
            return 0

        lax.fori_loop(0, span // 64, move, 0)
        row += span

    def clear(i, _):
        if carried:
            out[i] = previous[i].astype(out.dtype)
        else:
            out[i] = jnp.zeros(out.shape[1:], out.dtype)
        return 0

    lax.fori_loop(0, out.shape[0], clear, 0)
    start = table[0, slots + group]
    stop = table[0, slots + group + 1]
    dims = (((0,), (0,)), ((), ())) if flipped else (((1,), (0,)), ((), ()))

    def advance(number, total):
        for step in range(unroll):
            index = start + number * unroll + step
            real = index < stop
            entry = table[0, jnp.minimum(index, stop - 1)]
            slot = entry & 255
            place = (entry >> 8) & 255
            origin = pl.multiple_of(((entry >> 16) & 255) * edge, edge)
            fresh = jnp.logical_and(real, (entry >> 24) == 1)
            product = lax.dot_general(
                tiles[slot], source[pl.ds(origin, edge)], dims, preferred_element_type=f32
            )
            product = product * real.astype(f32)
            if carried:
                total = jnp.where(fresh, previous[place], total) + product
            else:
                total = total * (1.0 - fresh.astype(f32)) + product
            out[place] = total.astype(out.dtype)
        return total

    steps = (stop - start + unroll - 1) // unroll
    lax.fori_loop(0, steps, advance, jnp.zeros(out.shape[1:], f32))


def group_products(table, tiles, pieces, count, group, flipped, previous=None, dtype=bf16):
    slots, edge, _ = tiles.shape
    arrays = [array for array, _, _ in pieces]
    spans = [(first, span) for _, first, span in pieces]
    width = arrays[0].shape[1]
    operands = [table, tiles] + arrays + ([] if previous is None else [previous])
    whole = pl.BlockSpec(memory_space=pltpu.VMEM)
    return pl.pallas_call(
        functools.partial(
            group_kernel,
            spans=spans,
            group=group,
            flipped=flipped,
            carried=previous is not None,
        ),
        out_shape=jax.ShapeDtypeStruct((count, edge, width), dtype),
        in_specs=[pl.BlockSpec(memory_space=pltpu.SMEM)] + [whole] * (len(operands) - 1),
        out_specs=whole,
        scratch_shapes=[pltpu.VMEM((sum(span for _, span in spans), width), bf16)],
        compiler_params=pltpu.CompilerParams(vmem_limit_bytes=8 << 20),
        cost_estimate=pl.CostEstimate(
            flops=2 * slots * edge * edge * width // 4,
            bytes_accessed=count * edge * width * 4,
            transcendentals=0,
        ),
        name=("backward" if flipped else "forward") + str(group),
    )(*operands)


def order_kernel(coords, place_info, tiles, forward, backward, *, per_owner):
    del tiles
    slots = coords.shape[0]
    shape = (slots, padded)
    own_col = place_info[0]
    own_row = place_info[1]
    live_count = place_info[2]
    number = lax.broadcasted_iota(jnp.int32, (slots, 1), 0)
    alive = number < live_count
    tile_row = coords[:, 0:1]
    tile_col = coords[:, 1:2]
    owner_row = ((tile_row.astype(f32) + 0.5) * (1.0 / per_owner)).astype(jnp.int32)
    owner_col = ((tile_col.astype(f32) + 0.5) * (1.0 / per_owner)).astype(jnp.int32)
    apart = owner_row ^ own_col
    part = tile_row - owner_row * per_owner
    core = apart & 1
    x = (apart >> x_bit) & 3
    z = (apart >> z_bit) & 3
    block = (z >> 1) * 8 + x * 2 + (z & 1)
    chunk = jnp.zeros_like(part)
    inner = jnp.zeros_like(part)
    breadth = jnp.zeros_like(part)
    for k, members in enumerate(chunks):
        for i, member in enumerate(members):
            chunk = jnp.where(part == member, k, chunk)
            inner = jnp.where(part == member, i, inner)
            breadth = jnp.where(part == member, len(members), breadth)
    row_apart = owner_col ^ own_row
    source_place = ((row_apart & 1) * 4 + (row_apart >> y_bit)) * per_owner
    source_place = source_place + tile_col - owner_col * per_owner
    forward_place = block * breadth + inner
    forward_key = (chunk * 2 + 1 - core) * 128 + forward_place
    backward_origin = (core * 16 + x * 4 + z) * breadth + inner
    backward_key = chunk * 128 + source_place

    lane = lax.broadcasted_iota(jnp.int32, shape, 1)
    sub = lax.broadcasted_iota(jnp.int32, shape, 0)
    limit = ((lane[0:1] - slots) * 128).astype(f32)
    lane_number = lane[0:1].astype(f32)

    def table(key, place, origin, groups, out):
        key = jnp.where(alive, key, 1 << 20).astype(f32)
        place = jnp.where(alive, place, 0)
        origin = jnp.where(alive, origin, 0)
        across = jnp.sum(jnp.where(lane == sub, key, 0.0), axis=0, keepdims=True)
        same = jnp.logical_and(across == key, lane < sub)
        ahead = jnp.logical_and(jnp.logical_or(across < key, same), lane < slots)
        rank = jnp.sum(jnp.where(ahead, 1.0, 0.0), axis=1, keepdims=True)
        repeats = jnp.sum(jnp.where(same, 1.0, 0.0), axis=1, keepdims=True)
        fresh = (repeats == 0.0).astype(jnp.int32)
        low = (number | (place << 8)).astype(f32)
        high = (origin | (fresh << 8)).astype(f32)
        hit = rank == lane_number
        low = jnp.sum(jnp.where(hit, low, 0.0), axis=0, keepdims=True).astype(jnp.int32)
        high = jnp.sum(jnp.where(hit, high, 0.0), axis=0, keepdims=True).astype(jnp.int32)
        bound = jnp.minimum(limit, groups * 128.0)
        bounds = jnp.sum(jnp.where(key < bound, 1.0, 0.0), axis=0, keepdims=True)
        out[...] = jnp.where(lane[0:1] < slots, low | (high << 16), bounds.astype(jnp.int32))

    table(forward_key, forward_place, source_place, 2 * len(chunks), forward)
    table(backward_key, source_place, backward_origin, len(chunks), backward)


def slot_tables(coords, live_count, own_col, own_row, per_owner, tiles):
    place_info = jnp.stack([own_col, own_row, live_count])
    whole = pl.BlockSpec(memory_space=pltpu.VMEM)
    result = jax.ShapeDtypeStruct((1, padded), jnp.int32)
    return pl.pallas_call(
        functools.partial(order_kernel, per_owner=per_owner),
        out_shape=(result, result),
        in_specs=[whole, pl.BlockSpec(memory_space=pltpu.SMEM), whole],
        out_specs=(whole, whole),
        compiler_params=pltpu.CompilerParams(vmem_limit_bytes=8 << 20),
        name="order",
    )(coords, place_info, tiles)


def gather_row(block, table):
    near, far = 1 << y_bit, 3 << y_bit
    rows = block.shape[0]
    half = rows // 2
    across = exchange(block, "row", 1)
    first, third = exchange(block, "row", near), exchange(block, "row", far)
    first_across, third_across = exchange(across, "row", near), exchange(across, "row", far)
    first_across, third_across = after((first_across, third_across), table)
    low = exchange(jnp.concatenate([first[:half], first_across[:half]], axis=0), "row", far)
    high = exchange(jnp.concatenate([third[half:], third_across[half:]], axis=0), "row", near)
    return [
        (block, 0, rows),
        (first, 0, rows),
        (low, 0, half),
        (high, 0, half),
        (third, 0, rows),
        (across, 0, rows),
        (first_across, 0, rows),
        (low, half, half),
        (high, half, half),
        (third_across, 0, rows),
    ]


def wide(value):
    return value.astype(f32)


def reduce_row(terms, share):
    near, far = 1 << y_bit, 3 << y_bit
    rows, width = terms.shape[2:]
    low, high = terms[0], terms[1]

    def send(value, mask):
        rounded = share.astype(bf16)
        message = jnp.concatenate([value.reshape(-1, width), rounded], axis=0)
        message = exchange(message, "row", mask)
        split = message.shape[0] - share.shape[0]
        return message[:split].reshape(value.shape), wide(rounded) + wide(message[split:])

    high_in = exchange(high[2:4], "row", far)
    low_in, share = send(low[1:3], near)
    high_next = exchange((wide(high[1]) + wide(high_in[0])).astype(bf16), "row", near)
    low_next, share = send((wide(low[3]) + wide(low_in[1])).astype(bf16), far)
    leaving = (wide(high[0]) + wide(high_in[1]) + wide(high_next)).astype(bf16)
    arrived, share = send(leaving, 1)
    return wide(low[0]) + wide(low_in[0]) + wide(low_next) + wide(arrived), share


def per_device(
    embedding, weight, grad_out, in_degree, out_degree, tile_edges, tile_coords, tile_count
):
    tiles = tile_edges[0, 0]
    n_row = lax.axis_size("row")
    n_col = lax.axis_size("col")
    own_row = lax.axis_index("row").astype(jnp.int32)
    own_col = lax.axis_index("col").astype(jnp.int32)
    own_rows, width = embedding.shape
    edge = tiles.shape[1]
    per_owner = own_rows // edge
    total_nodes = own_rows * n_row * n_col

    scale_out = lax.rsqrt(out_degree.astype(f32))
    scale_in = lax.rsqrt(in_degree.astype(f32))
    scaled = (scale_out[:, None] * wide(embedding)).astype(bf16)
    forward_table, backward_table = slot_tables(
        tile_coords[0, 0], tile_count[0, 0], own_col, own_row, per_owner, tiles
    )
    source = gather_row(scaled, forward_table)

    near, far = 1 << x_bit, 3 << x_bit
    z = (own_col >> z_bit) & 3
    share_rows = width // 4
    number = range(len(chunks))
    heights = [len(members) * edge for members in chunks]

    def own(k, value):
        return jnp.concatenate([value[m * edge : (m + 1) * edge] for m in chunks[k]], axis=0)

    first_messages = []
    both = []
    for k in number:
        table = after(forward_table, first_messages[-1]) if k else forward_table
        count = 16 * len(chunks[k])
        shape = (2, 4, 2, heights[k], width)
        leaving = group_products(table, tiles, source, count, 2 * k, False)
        core_in = exchange(leaving, "col", 1).reshape(shape)
        kept = group_products(table, tiles, source, count, 2 * k + 1, False).reshape(shape)

        def sums(half, low, high, kept=kept, core_in=core_in):
            return wide(kept[half, low:high]) + wide(core_in[half, low:high])

        both.append(sums)
        first_messages.append((sums(0, 1, 3).astype(bf16), sums(1, 2, 4).astype(bf16)))
    reduced = []
    second_messages = None
    all_second = []
    for k in number:
        messages = first_messages[k]
        if k:
            messages = after(messages, second_messages)
        low_in = exchange(messages[0], "col", near)
        high_in = exchange(messages[1], "col", far)
        low_in, high_in = lax.optimization_barrier((low_in, high_in))
        second_messages = (
            (both[k](0, 3, 4)[0] + wide(low_in[1])).astype(bf16),
            (both[k](1, 1, 2)[0] + wide(high_in[0])).astype(bf16),
        )
        second_messages = lax.optimization_barrier(second_messages)
        all_second.append(second_messages)
        low_next = exchange(second_messages[0], "col", far)
        high_next = exchange(second_messages[1], "col", near)
        low = both[k](0, 0, 1)[0] + wide(low_in[0]) + wide(low_next)
        high = both[k](1, 0, 1)[0] + wide(high_in[1]) + wide(high_next)
        blocks = (low[0], low[1].astype(bf16), high[0].astype(bf16), high[1].astype(bf16))
        reduced.append(after(blocks, first_messages[k + 1 :]))

    hidden_parts = []
    local_weight = jnp.zeros((width, width), f32)
    stacks = []
    upstream = None
    for k in number:
        rows = heights[k]
        last = k == len(chunks) - 1
        blocks = reduced[k]
        if k:
            blocks = after(blocks, upstream)
        summed = blocks[0]
        for distance in (1, 2, 3):
            summed = summed + wide(exchange(blocks[distance], "col", distance << z_bit))
        if k:
            summed = after(summed, stacks[-1])
        chunk_scale = own(k, scale_in)
        aggregate = (chunk_scale[:, None] * summed).astype(bf16)
        preact = jnp.dot(aggregate, weight, preferred_element_type=f32)
        gates = jax.nn.sigmoid(preact)
        hidden_parts.append((preact * gates).astype(bf16))
        delta = (wide(own(k, grad_out)) * gates * (1.0 + preact * (1.0 - gates))).astype(bf16)
        local_weight = local_weight + lax.dot_general(
            aggregate, delta, (((0,), (0,)), ((), ())), preferred_element_type=f32
        )
        projected = lax.dot_general(
            delta, weight, (((1,), (1,)), ((), ())), preferred_element_type=f32
        )
        upstream = (chunk_scale[:, None] * projected).astype(bf16)

        def weight_share(distance):
            return lax.dynamic_slice_in_dim(
                local_weight, (z ^ distance) * share_rows, share_rows, 0
            )

        stack = [upstream]
        if last:
            share = weight_share(0)
        for distance in (1, 2, 3):
            message = upstream
            if last:
                message = jnp.concatenate([upstream, weight_share(distance).astype(bf16)], axis=0)
            message = exchange(message, "col", distance << z_bit)
            stack.append(message[:rows])
            if last:
                share = share + wide(message[rows:])
        if last:
            stack.append(share.astype(bf16))
        stacks.append(after(jnp.concatenate(stack, axis=0), all_second[k + 1 :]))

    terms = None
    for k in number:
        rows = heights[k]
        last = k == len(chunks) - 1
        stack = stacks[k]
        if k:
            stack = after(stack, (second_low, second_high))
        first = exchange(stack, "col", near)
        third = exchange(stack, "col", far)
        if k:
            terms = products(k - 1)
            first, third = after((first, third), terms)
        low = first[: 2 * rows]
        if last:
            low = jnp.concatenate([low, first[4 * rows :]], axis=0)
        second_low = exchange(low, "col", far)
        second_high = exchange(third[2 * rows : 4 * rows], "col", near)
        if last:
            share = (wide(stack[4 * rows :]) + wide(first[4 * rows :])) + (
                wide(second_low[2 * rows :]) + wide(third[4 * rows :])
            )
        blocks = [stack[: 4 * rows], first[: 4 * rows], third[: 4 * rows]]
        seconds = [second_low[: 2 * rows], second_high]
        pieces = [
            (stack, 0, 4 * rows),
            (first, 0, 4 * rows),
            (second_low, 0, 2 * rows),
            (second_high, 0, 2 * rows),
            (third, 0, 4 * rows),
        ]

        def products(
            k, last=last, rows=rows, pieces=pieces, blocks=blocks, seconds=seconds, terms=terms
        ):
            if last:
                main = exchange(jnp.concatenate(blocks, axis=0), "col", 1)
                second, base = exchange(jnp.concatenate(seconds, axis=0), "col", 1), 0
            else:
                main = exchange(jnp.concatenate(blocks + seconds, axis=0), "col", 1)
                second, base = main, 12 * rows
            arrived = [
                (main, 0, 4 * rows),
                (main, 4 * rows, 4 * rows),
                (second, base, 2 * rows),
                (second, base + 2 * rows, 2 * rows),
                (main, 8 * rows, 4 * rows),
            ]
            return group_products(
                backward_table,
                tiles,
                pieces + arrived,
                n_row * per_owner,
                k,
                True,
                terms,
                bf16 if last else f32,
            )

    share = share + exchange(share, "col", 1)
    terms = products(len(chunks) - 1)
    source_total, share = reduce_row(terms.reshape(2, 4, own_rows, width), share)
    share = share.astype(bf16)
    grad_weight = jnp.zeros((width, width), f32)
    for distance in (0, 1, 2, 3):
        piece = exchange(share, "col", distance << z_bit) if distance else share
        grad_weight = lax.dynamic_update_slice_in_dim(
            grad_weight, wide(piece), (z ^ distance) * share_rows, 0
        )
    grad_weight = grad_weight / math.sqrt(total_nodes)
    decay = decay_rate * jnp.sqrt(out_degree.astype(f32))
    grad_embedding = scale_out[:, None] * source_total + decay[:, None] * wide(embedding)

    hidden = jnp.concatenate(hidden_parts, axis=0)
    return (hidden, grad_embedding, grad_weight)


def solution(mesh):
    in_specs = (
        P(("col", "row"), None),
        P(),
        P(("row", "col"), None),
        P(("row", "col")),
        P(("col", "row")),
        P("row", "col", None, None, None),
        P("row", "col", None, None),
        P("row", "col"),
    )
    out_specs = (P(("row", "col"), None), P(("col", "row"), None), P())
    return jax.shard_map(
        per_device, mesh=mesh, in_specs=in_specs, out_specs=out_specs, check_vma=False
    )
```

```python
import functools
import math

import jax
import jax.numpy as jnp
from jax import lax
from jax.experimental import pallas as pl
from jax.experimental.pallas import tpu as pltpu
from jax.sharding import PartitionSpec as P

decay_rate = 0.01
f32 = jnp.float32
bf16 = jnp.bfloat16

chunks = ((0,), (1, 2))
unroll = 8
padded = 256

x_bit, z_bit, y_bit = 1, 3, 1


def exchange(value, axis, mask):
    size = lax.axis_size(axis)
    return lax.ppermute(value, axis, [(i, i ^ mask) for i in range(size)])


def after(value, earlier):
    return lax.optimization_barrier((value, earlier))[0]


def group_kernel(table, tiles, *rest, spans, group, flipped, carried):
    pieces = rest[: len(spans)]
    previous = rest[len(spans)] if carried else None
    out, source = rest[-2:]
    slots, edge, _ = tiles.shape
    row = 0
    for piece, (first, span) in zip(pieces, spans):

        def move(i, _, piece=piece, row=row, first=first):
            source[pl.ds(row + i * 64, 64)] = piece[pl.ds(first + i * 64, 64)]
            return 0

        lax.fori_loop(0, span // 64, move, 0)
        row += span

    def clear(i, _):
        if carried:
            out[i] = previous[i].astype(out.dtype)
        else:
            out[i] = jnp.zeros(out.shape[1:], out.dtype)
        return 0

    lax.fori_loop(0, out.shape[0], clear, 0)
    start = table[0, slots + group]
    stop = table[0, slots + group + 1]
    dims = (((0,), (0,)), ((), ())) if flipped else (((1,), (0,)), ((), ()))

    def advance(number, total):
        for step in range(unroll):
            index = start + number * unroll + step
            real = index < stop
            entry = table[0, jnp.minimum(index, stop - 1)]
            slot = entry & 255
            place = (entry >> 8) & 255
            origin = pl.multiple_of(((entry >> 16) & 255) * edge, edge)
            fresh = jnp.logical_and(real, (entry >> 24) == 1)
            product = lax.dot_general(
                tiles[slot], source[pl.ds(origin, edge)], dims, preferred_element_type=f32
            )
            product = product * real.astype(f32)
            if carried:
                total = jnp.where(fresh, previous[place], total) + product
            else:
                total = total * (1.0 - fresh.astype(f32)) + product
            out[place] = total.astype(out.dtype)
        return total

    steps = (stop - start + unroll - 1) // unroll
    lax.fori_loop(0, steps, advance, jnp.zeros(out.shape[1:], f32))


def group_products(table, tiles, pieces, count, group, flipped, previous=None, dtype=bf16):
    slots, edge, _ = tiles.shape
    arrays = [array for array, _, _ in pieces]
    spans = [(first, span) for _, first, span in pieces]
    width = arrays[0].shape[1]
    operands = [table, tiles] + arrays + ([] if previous is None else [previous])
    whole = pl.BlockSpec(memory_space=pltpu.VMEM)
    return pl.pallas_call(
        functools.partial(
            group_kernel,
            spans=spans,
            group=group,
            flipped=flipped,
            carried=previous is not None,
        ),
        out_shape=jax.ShapeDtypeStruct((count, edge, width), dtype),
        in_specs=[pl.BlockSpec(memory_space=pltpu.SMEM)] + [whole] * (len(operands) - 1),
        out_specs=whole,
        scratch_shapes=[pltpu.VMEM((sum(span for _, span in spans), width), bf16)],
        compiler_params=pltpu.CompilerParams(vmem_limit_bytes=8 << 20),
        cost_estimate=pl.CostEstimate(
            flops=2 * slots * edge * edge * width // 4,
            bytes_accessed=count * edge * width * 4,
            transcendentals=0,
        ),
        name=("backward" if flipped else "forward") + str(group),
    )(*operands)


def order_kernel(coords, place_info, tiles, forward, backward, *, per_owner):
    del tiles
    slots = coords.shape[0]
    shape = (slots, padded)
    own_col = place_info[0]
    own_row = place_info[1]
    live_count = place_info[2]
    number = lax.broadcasted_iota(jnp.int32, (slots, 1), 0)
    alive = number < live_count
    tile_row = coords[:, 0:1]
    tile_col = coords[:, 1:2]
    owner_row = ((tile_row.astype(f32) + 0.5) * (1.0 / per_owner)).astype(jnp.int32)
    owner_col = ((tile_col.astype(f32) + 0.5) * (1.0 / per_owner)).astype(jnp.int32)
    apart = owner_row ^ own_col
    part = tile_row - owner_row * per_owner
    core = apart & 1
    x = (apart >> x_bit) & 3
    z = (apart >> z_bit) & 3
    block = (z >> 1) * 8 + x * 2 + (z & 1)
    chunk = jnp.zeros_like(part)
    inner = jnp.zeros_like(part)
    breadth = jnp.zeros_like(part)
    for k, members in enumerate(chunks):
        for i, member in enumerate(members):
            chunk = jnp.where(part == member, k, chunk)
            inner = jnp.where(part == member, i, inner)
            breadth = jnp.where(part == member, len(members), breadth)
    row_apart = owner_col ^ own_row
    source_place = ((row_apart & 1) * 4 + (row_apart >> y_bit)) * per_owner
    source_place = source_place + tile_col - owner_col * per_owner
    forward_place = block * breadth + inner
    forward_key = (chunk * 2 + 1 - core) * 128 + forward_place
    backward_origin = (core * 16 + x * 4 + z) * breadth + inner
    backward_key = chunk * 128 + source_place

    lane = lax.broadcasted_iota(jnp.int32, shape, 1)
    sub = lax.broadcasted_iota(jnp.int32, shape, 0)
    limit = ((lane[0:1] - slots) * 128).astype(f32)
    lane_number = lane[0:1].astype(f32)

    def table(key, place, origin, groups, out):
        key = jnp.where(alive, key, 1 << 20).astype(f32)
        place = jnp.where(alive, place, 0)
        origin = jnp.where(alive, origin, 0)
        across = jnp.sum(jnp.where(lane == sub, key, 0.0), axis=0, keepdims=True)
        same = jnp.logical_and(across == key, lane < sub)
        ahead = jnp.logical_and(jnp.logical_or(across < key, same), lane < slots)
        rank = jnp.sum(jnp.where(ahead, 1.0, 0.0), axis=1, keepdims=True)
        repeats = jnp.sum(jnp.where(same, 1.0, 0.0), axis=1, keepdims=True)
        fresh = (repeats == 0.0).astype(jnp.int32)
        low = (number | (place << 8)).astype(f32)
        high = (origin | (fresh << 8)).astype(f32)
        hit = rank == lane_number
        low = jnp.sum(jnp.where(hit, low, 0.0), axis=0, keepdims=True).astype(jnp.int32)
        high = jnp.sum(jnp.where(hit, high, 0.0), axis=0, keepdims=True).astype(jnp.int32)
        bound = jnp.minimum(limit, groups * 128.0)
        bounds = jnp.sum(jnp.where(key < bound, 1.0, 0.0), axis=0, keepdims=True)
        out[...] = jnp.where(lane[0:1] < slots, low | (high << 16), bounds.astype(jnp.int32))

    table(forward_key, forward_place, source_place, 2 * len(chunks), forward)
    table(backward_key, source_place, backward_origin, len(chunks), backward)


def slot_tables(coords, live_count, own_col, own_row, per_owner, tiles):
    place_info = jnp.stack([own_col, own_row, live_count])
    whole = pl.BlockSpec(memory_space=pltpu.VMEM)
    result = jax.ShapeDtypeStruct((1, padded), jnp.int32)
    return pl.pallas_call(
        functools.partial(order_kernel, per_owner=per_owner),
        out_shape=(result, result),
        in_specs=[whole, pl.BlockSpec(memory_space=pltpu.SMEM), whole],
        out_specs=(whole, whole),
        compiler_params=pltpu.CompilerParams(vmem_limit_bytes=8 << 20),
        name="order",
    )(coords, place_info, tiles)


def gather_row(block):
    near, far = 1 << y_bit, 3 << y_bit
    rows = block.shape[0]
    half = rows // 2
    across = exchange(block, "row", 1)
    first, third = exchange(block, "row", near), exchange(block, "row", far)
    first_across, third_across = exchange(across, "row", near), exchange(across, "row", far)
    low = jnp.concatenate([first[:half], first_across[:half]], axis=0)
    high = jnp.concatenate([third[half:], third_across[half:]], axis=0)
    messages = lax.optimization_barrier((low, high))
    low = exchange(messages[0], "row", far)
    high = exchange(messages[1], "row", near)
    return messages, [
        (block, 0, rows),
        (first, 0, rows),
        (low, 0, half),
        (high, 0, half),
        (third, 0, rows),
        (across, 0, rows),
        (first_across, 0, rows),
        (low, half, half),
        (high, half, half),
        (third_across, 0, rows),
    ]


def wide(value):
    return value.astype(f32)


def reduce_row(terms, share):
    near, far = 1 << y_bit, 3 << y_bit
    rows, width = terms.shape[2:]
    low, high = terms[0], terms[1]

    def send(value, mask):
        rounded = share.astype(bf16)
        message = jnp.concatenate([value.reshape(-1, width), rounded], axis=0)
        message = exchange(message, "row", mask)
        split = message.shape[0] - share.shape[0]
        return message[:split].reshape(value.shape), wide(rounded) + wide(message[split:])

    high_in = exchange(high[2:4], "row", far)
    low_in, share = send(low[1:3], near)
    high_next = exchange((wide(high[1]) + wide(high_in[0])).astype(bf16), "row", near)
    low_next, share = send((wide(low[3]) + wide(low_in[1])).astype(bf16), far)
    leaving = (wide(high[0]) + wide(high_in[1]) + wide(high_next)).astype(bf16)
    arrived, share = send(leaving, 1)
    return wide(low[0]) + wide(low_in[0]) + wide(low_next) + wide(arrived), share


def per_device(
    embedding, weight, grad_out, in_degree, out_degree, tile_edges, tile_coords, tile_count
):
    tiles = tile_edges[0, 0]
    n_row = lax.axis_size("row")
    n_col = lax.axis_size("col")
    own_row = lax.axis_index("row").astype(jnp.int32)
    own_col = lax.axis_index("col").astype(jnp.int32)
    own_rows, width = embedding.shape
    edge = tiles.shape[1]
    per_owner = own_rows // edge
    total_nodes = own_rows * n_row * n_col

    scale_out = lax.rsqrt(out_degree.astype(f32))
    scale_in = lax.rsqrt(in_degree.astype(f32))
    scaled = (scale_out[:, None] * wide(embedding)).astype(bf16)
    messages, source = gather_row(scaled)
    coords = after(tile_coords[0, 0], messages)
    forward_table, backward_table = slot_tables(
        coords, tile_count[0, 0], own_col, own_row, per_owner, tiles
    )

    near, far = 1 << x_bit, 3 << x_bit
    z = (own_col >> z_bit) & 3
    share_rows = width // 4
    number = range(len(chunks))
    heights = [len(members) * edge for members in chunks]

    def own(k, value):
        return jnp.concatenate([value[m * edge : (m + 1) * edge] for m in chunks[k]], axis=0)

    first_messages = []
    both = []
    for k in number:
        table = after(forward_table, first_messages[-1]) if k else forward_table
        count = 16 * len(chunks[k])
        shape = (2, 4, 2, heights[k], width)
        leaving = group_products(table, tiles, source, count, 2 * k, False)
        core_in = exchange(leaving, "col", 1).reshape(shape)
        kept = group_products(table, tiles, source, count, 2 * k + 1, False).reshape(shape)

        def sums(half, low, high, kept=kept, core_in=core_in):
            return wide(kept[half, low:high]) + wide(core_in[half, low:high])

        both.append(sums)
        first_messages.append((sums(0, 1, 3).astype(bf16), sums(1, 2, 4).astype(bf16)))
    reduced = []
    second_messages = None
    all_second = []
    for k in number:
        messages = first_messages[k]
        if k:
            messages = after(messages, second_messages)
        low_in = exchange(messages[0], "col", near)
        high_in = exchange(messages[1], "col", far)
        low_in, high_in = lax.optimization_barrier((low_in, high_in))
        second_messages = (
            (both[k](0, 3, 4)[0] + wide(low_in[1])).astype(bf16),
            (both[k](1, 1, 2)[0] + wide(high_in[0])).astype(bf16),
        )
        second_messages = lax.optimization_barrier(second_messages)
        all_second.append(second_messages)
        low_next = exchange(second_messages[0], "col", far)
        high_next = exchange(second_messages[1], "col", near)
        low = both[k](0, 0, 1)[0] + wide(low_in[0]) + wide(low_next)
        high = both[k](1, 0, 1)[0] + wide(high_in[1]) + wide(high_next)
        blocks = (low[0], low[1].astype(bf16), high[0].astype(bf16), high[1].astype(bf16))
        reduced.append(after(blocks, first_messages[k + 1 :]))

    hidden_parts = []
    local_weight = jnp.zeros((width, width), f32)
    stacks = []
    upstream = None
    for k in number:
        rows = heights[k]
        last = k == len(chunks) - 1
        blocks = reduced[k]
        if k:
            blocks = after(blocks, upstream)
        summed = blocks[0]
        for distance in (1, 2, 3):
            summed = summed + wide(exchange(blocks[distance], "col", distance << z_bit))
        if k:
            summed = after(summed, stacks[-1])
        chunk_scale = own(k, scale_in)
        aggregate = (chunk_scale[:, None] * summed).astype(bf16)
        preact = jnp.dot(aggregate, weight, preferred_element_type=f32)
        gates = jax.nn.sigmoid(preact)
        hidden_parts.append((preact * gates).astype(bf16))
        delta = (wide(own(k, grad_out)) * gates * (1.0 + preact * (1.0 - gates))).astype(bf16)
        local_weight = local_weight + lax.dot_general(
            aggregate, delta, (((0,), (0,)), ((), ())), preferred_element_type=f32
        )
        projected = lax.dot_general(
            delta, weight, (((1,), (1,)), ((), ())), preferred_element_type=f32
        )
        upstream = (chunk_scale[:, None] * projected).astype(bf16)

        def weight_share(distance):
            return lax.dynamic_slice_in_dim(
                local_weight, (z ^ distance) * share_rows, share_rows, 0
            )

        stack = [upstream]
        messages = (upstream,) * 3
        if last:
            share = weight_share(0)
            messages = lax.optimization_barrier(
                tuple(
                    jnp.concatenate([upstream, weight_share(d).astype(bf16)], axis=0)
                    for d in (1, 2, 3)
                )
            )
        for distance, message in zip((1, 2, 3), messages):
            message = exchange(message, "col", distance << z_bit)
            stack.append(message[:rows])
            if last:
                share = share + wide(message[rows:])
        if last:
            stack.append(share.astype(bf16))
        stacks.append(after(jnp.concatenate(stack, axis=0), all_second[k + 1 :]))

    terms = None
    for k in number:
        rows = heights[k]
        last = k == len(chunks) - 1
        stack = stacks[k]
        if k:
            stack = after(stack, (second_low, second_high))
        first = exchange(stack, "col", near)
        third = exchange(stack, "col", far)
        if not last:
            first, third = after((first, third), messages)
        if k:
            terms = products(k - 1)
            first, third = after((first, third), terms)
        low = first[: 2 * rows]
        if last:
            low = jnp.concatenate([low, first[4 * rows :]], axis=0)
        second_low = exchange(low, "col", far)
        second_high = exchange(third[2 * rows : 4 * rows], "col", near)
        if last:
            share = (wide(stack[4 * rows :]) + wide(first[4 * rows :])) + (
                wide(second_low[2 * rows :]) + wide(third[4 * rows :])
            )
        blocks = [stack[: 4 * rows], first[: 4 * rows], third[: 4 * rows]]
        seconds = [second_low[: 2 * rows], second_high]
        pieces = [
            (stack, 0, 4 * rows),
            (first, 0, 4 * rows),
            (second_low, 0, 2 * rows),
            (second_high, 0, 2 * rows),
            (third, 0, 4 * rows),
        ]

        def products(
            k, last=last, rows=rows, pieces=pieces, blocks=blocks, seconds=seconds, terms=terms
        ):
            if last:
                main = exchange(jnp.concatenate(blocks, axis=0), "col", 1)
                second, base = exchange(jnp.concatenate(seconds, axis=0), "col", 1), 0
            else:
                main = exchange(jnp.concatenate(blocks + seconds, axis=0), "col", 1)
                second, base = main, 12 * rows
            arrived = [
                (main, 0, 4 * rows),
                (main, 4 * rows, 4 * rows),
                (second, base, 2 * rows),
                (second, base + 2 * rows, 2 * rows),
                (main, 8 * rows, 4 * rows),
            ]
            return group_products(
                backward_table,
                tiles,
                pieces + arrived,
                n_row * per_owner,
                k,
                True,
                terms,
                bf16 if last else f32,
            )

    share = share + exchange(share, "col", 1)
    terms = products(len(chunks) - 1)
    source_total, share = reduce_row(terms.reshape(2, 4, own_rows, width), share)
    share = share.astype(bf16)
    grad_weight = jnp.zeros((width, width), f32)
    for distance in (0, 1, 2, 3):
        piece = exchange(share, "col", distance << z_bit) if distance else share
        grad_weight = lax.dynamic_update_slice_in_dim(
            grad_weight, wide(piece), (z ^ distance) * share_rows, 0
        )
    grad_weight = grad_weight / math.sqrt(total_nodes)
    decay = decay_rate * jnp.sqrt(out_degree.astype(f32))
    grad_embedding = scale_out[:, None] * source_total + decay[:, None] * wide(embedding)

    hidden = jnp.concatenate(hidden_parts, axis=0)
    return (hidden, grad_embedding, grad_weight)


def solution(mesh):
    in_specs = (
        P(("col", "row"), None),
        P(),
        P(("row", "col"), None),
        P(("row", "col")),
        P(("col", "row")),
        P("row", "col", None, None, None),
        P("row", "col", None, None),
        P("row", "col"),
    )
    out_specs = (P(("row", "col"), None), P(("col", "row"), None), P())
    return jax.shard_map(
        per_device, mesh=mesh, in_specs=in_specs, out_specs=out_specs, check_vma=False
    )
```

```python
import functools
import math

import jax
import jax.numpy as jnp
from jax import lax
from jax.experimental import pallas as pl
from jax.experimental.pallas import tpu as pltpu
from jax.sharding import PartitionSpec as P

decay_rate = 0.01
f32 = jnp.float32
bf16 = jnp.bfloat16

chunks = ((0,), (1, 2))
forward_unroll = 8
backward_unroll = 16
padded = 256

x_bit, z_bit, y_bit = 1, 3, 1


def exchange(value, axis, mask):
    size = lax.axis_size(axis)
    return lax.ppermute(value, axis, [(i, i ^ mask) for i in range(size)])


def after(value, earlier):
    return lax.optimization_barrier((value, earlier))[0]


def group_kernel(table, tiles, *rest, spans, group, flipped, carried, base):
    unroll = backward_unroll if flipped else forward_unroll
    pieces = rest[: len(spans)]
    previous = rest[len(spans)] if carried else None
    out, source = rest[-2:]
    slots, edge, _ = tiles.shape
    row = 0
    for piece, (first, span) in zip(pieces, spans):

        def move(i, _, piece=piece, row=row, first=first):
            source[pl.ds(row + i * 64, 64)] = piece[pl.ds(first + i * 64, 64)]
            return 0

        lax.fori_loop(0, span // 64, move, 0)
        row += span

    def clear(i, _):
        if carried:
            out[i] = previous[base + i].astype(out.dtype)
        else:
            out[i] = jnp.zeros(out.shape[1:], out.dtype)
        return 0

    lax.fori_loop(0, out.shape[0], clear, 0)
    start = table[0, slots + group]
    stop = table[0, slots + group + 1]
    dims = (((0,), (0,)), ((), ())) if flipped else (((1,), (0,)), ((), ()))

    def advance(number, total):
        for step in range(unroll):
            index = start + number * unroll + step
            real = index < stop
            entry = table[0, jnp.minimum(index, stop - 1)]
            slot = entry & 255
            place = (entry >> 8) & 255
            origin = pl.multiple_of(((entry >> 16) & 255) * edge, edge)
            fresh = jnp.logical_and(real, (entry >> 24) == 1)
            product = lax.dot_general(
                tiles[slot], source[pl.ds(origin, edge)], dims, preferred_element_type=f32
            )
            product = product * real.astype(f32)
            if carried:
                total = jnp.where(fresh, previous[place], total) + product
            else:
                total = total * (1.0 - fresh.astype(f32)) + product
            out[place - base] = total.astype(out.dtype)
        return total

    steps = (stop - start + unroll - 1) // unroll
    lax.fori_loop(0, steps, advance, jnp.zeros(out.shape[1:], f32))


def group_products(
    table, tiles, pieces, count, group, flipped, previous=None, dtype=bf16, base=0
):
    slots, edge, _ = tiles.shape
    arrays = [array for array, _, _ in pieces]
    spans = [(first, span) for _, first, span in pieces]
    width = arrays[0].shape[1]
    operands = [table, tiles] + arrays + ([] if previous is None else [previous])
    whole = pl.BlockSpec(memory_space=pltpu.VMEM)
    return pl.pallas_call(
        functools.partial(
            group_kernel,
            spans=spans,
            group=group,
            flipped=flipped,
            carried=previous is not None,
            base=base,
        ),
        out_shape=jax.ShapeDtypeStruct((count, edge, width), dtype),
        in_specs=[pl.BlockSpec(memory_space=pltpu.SMEM)] + [whole] * (len(operands) - 1),
        out_specs=whole,
        scratch_shapes=[pltpu.VMEM((sum(span for _, span in spans), width), bf16)],
        compiler_params=pltpu.CompilerParams(vmem_limit_bytes=8 << 20),
        cost_estimate=pl.CostEstimate(
            flops=2 * slots * edge * edge * width // 4,
            bytes_accessed=count * edge * width * 4,
            transcendentals=0,
        ),
        name=("backward" if flipped else "forward") + str(group),
    )(*operands)


def order_kernel(coords, place_info, tiles, forward, backward, *, per_owner):
    del tiles
    slots = coords.shape[0]
    shape = (slots, padded)
    own_col = place_info[0]
    own_row = place_info[1]
    live_count = place_info[2]
    number = lax.broadcasted_iota(jnp.int32, (slots, 1), 0)
    alive = number < live_count
    tile_row = coords[:, 0:1]
    tile_col = coords[:, 1:2]
    owner_row = ((tile_row.astype(f32) + 0.5) * (1.0 / per_owner)).astype(jnp.int32)
    owner_col = ((tile_col.astype(f32) + 0.5) * (1.0 / per_owner)).astype(jnp.int32)
    apart = owner_row ^ own_col
    part = tile_row - owner_row * per_owner
    core = apart & 1
    x = (apart >> x_bit) & 3
    z = (apart >> z_bit) & 3
    block = (z >> 1) * 8 + x * 2 + (z & 1)
    chunk = jnp.zeros_like(part)
    inner = jnp.zeros_like(part)
    breadth = jnp.zeros_like(part)
    for k, members in enumerate(chunks):
        for i, member in enumerate(members):
            chunk = jnp.where(part == member, k, chunk)
            inner = jnp.where(part == member, i, inner)
            breadth = jnp.where(part == member, len(members), breadth)
    row_apart = owner_col ^ own_row
    source_place = ((row_apart & 1) * 4 + (row_apart >> y_bit)) * per_owner
    source_place = source_place + tile_col - owner_col * per_owner
    forward_place = block * breadth + inner
    forward_key = (chunk * 2 + 1 - core) * 128 + forward_place
    backward_origin = (core * 16 + x * 4 + z) * breadth + inner
    kept = jnp.logical_and(chunk == len(chunks) - 1, (row_apart & 1) == 0)
    backward_key = (chunk + kept.astype(jnp.int32)) * 128 + source_place

    lane = lax.broadcasted_iota(jnp.int32, shape, 1)
    sub = lax.broadcasted_iota(jnp.int32, shape, 0)
    limit = ((lane[0:1] - slots) * 128).astype(f32)
    lane_number = lane[0:1].astype(f32)

    def table(key, place, origin, groups, out):
        key = jnp.where(alive, key, 1 << 20).astype(f32)
        place = jnp.where(alive, place, 0)
        origin = jnp.where(alive, origin, 0)
        across = jnp.sum(jnp.where(lane == sub, key, 0.0), axis=0, keepdims=True)
        same = jnp.logical_and(across == key, lane < sub)
        ahead = jnp.logical_and(jnp.logical_or(across < key, same), lane < slots)
        rank = jnp.sum(jnp.where(ahead, 1.0, 0.0), axis=1, keepdims=True)
        repeats = jnp.sum(jnp.where(same, 1.0, 0.0), axis=1, keepdims=True)
        fresh = (repeats == 0.0).astype(jnp.int32)
        low = (number | (place << 8)).astype(f32)
        high = (origin | (fresh << 8)).astype(f32)
        hit = rank == lane_number
        low = jnp.sum(jnp.where(hit, low, 0.0), axis=0, keepdims=True).astype(jnp.int32)
        high = jnp.sum(jnp.where(hit, high, 0.0), axis=0, keepdims=True).astype(jnp.int32)
        bound = jnp.minimum(limit, groups * 128.0)
        bounds = jnp.sum(jnp.where(key < bound, 1.0, 0.0), axis=0, keepdims=True)
        out[...] = jnp.where(lane[0:1] < slots, low | (high << 16), bounds.astype(jnp.int32))

    table(forward_key, forward_place, source_place, 2 * len(chunks), forward)
    table(backward_key, source_place, backward_origin, len(chunks) + 1, backward)


def slot_tables(coords, live_count, own_col, own_row, per_owner, tiles):
    place_info = jnp.stack([own_col, own_row, live_count])
    whole = pl.BlockSpec(memory_space=pltpu.VMEM)
    result = jax.ShapeDtypeStruct((1, padded), jnp.int32)
    return pl.pallas_call(
        functools.partial(order_kernel, per_owner=per_owner),
        out_shape=(result, result),
        in_specs=[whole, pl.BlockSpec(memory_space=pltpu.SMEM), whole],
        out_specs=(whole, whole),
        compiler_params=pltpu.CompilerParams(vmem_limit_bytes=8 << 20),
        name="order",
    )(coords, place_info, tiles)


def gather_row(block):
    near, far = 1 << y_bit, 3 << y_bit
    rows = block.shape[0]
    half = rows // 2
    across = exchange(block, "row", 1)
    first, third = exchange(block, "row", near), exchange(block, "row", far)
    first_across, third_across = exchange(across, "row", near), exchange(across, "row", far)
    low = jnp.concatenate([first[:half], first_across[:half]], axis=0)
    high = jnp.concatenate([third[half:], third_across[half:]], axis=0)
    messages = lax.optimization_barrier((low, high))
    low = exchange(messages[0], "row", far)
    high = exchange(messages[1], "row", near)
    return messages, [
        (block, 0, rows),
        (first, 0, rows),
        (low, 0, half),
        (high, 0, half),
        (third, 0, rows),
        (across, 0, rows),
        (first_across, 0, rows),
        (low, half, half),
        (high, half, half),
        (third_across, 0, rows),
    ]


def wide(value):
    return value.astype(f32)


def reduce_row(low, high, share):
    near, far = 1 << y_bit, 3 << y_bit
    width = low.shape[2]

    def send(value, mask):
        rounded = share.astype(bf16)
        message = jnp.concatenate([value.reshape(-1, width), rounded], axis=0)
        message = exchange(message, "row", mask)
        split = message.shape[0] - share.shape[0]
        return message[:split].reshape(value.shape), wide(rounded) + wide(message[split:])

    high_in = exchange(high[2:4], "row", far)
    low_in, share = send(low[1:3], near)
    high_second = (wide(high[1]) + wide(high_in[0])).astype(bf16)
    high_next = exchange(high_second, "row", near)
    low_second = (wide(low[3]) + wide(low_in[1])).astype(bf16)
    low_next, share = send(after(low_second, high_second), far)
    leaving = (wide(high[0]) + wide(high_in[1]) + wide(high_next)).astype(bf16)
    arrived = exchange(leaving, "row", 1)
    total = wide(low[0]) + wide(low_in[0]) + wide(low_next) + wide(arrived)
    return total, after(share, leaving)


def per_device(
    embedding, weight, grad_out, in_degree, out_degree, tile_edges, tile_coords, tile_count
):
    tiles = tile_edges[0, 0]
    n_row = lax.axis_size("row")
    n_col = lax.axis_size("col")
    own_row = lax.axis_index("row").astype(jnp.int32)
    own_col = lax.axis_index("col").astype(jnp.int32)
    own_rows, width = embedding.shape
    edge = tiles.shape[1]
    per_owner = own_rows // edge
    total_nodes = own_rows * n_row * n_col

    scale_out = lax.rsqrt(out_degree.astype(f32))
    scale_in = lax.rsqrt(in_degree.astype(f32))
    scaled = (scale_out[:, None] * wide(embedding)).astype(bf16)
    messages, source = gather_row(scaled)
    coords = after(tile_coords[0, 0], messages)
    forward_table, backward_table = slot_tables(
        coords, tile_count[0, 0], own_col, own_row, per_owner, tiles
    )

    near, far = 1 << x_bit, 3 << x_bit
    z = (own_col >> z_bit) & 3
    share_rows = width // 4
    number = range(len(chunks))
    heights = [len(members) * edge for members in chunks]

    def own(k, value):
        return jnp.concatenate([value[m * edge : (m + 1) * edge] for m in chunks[k]], axis=0)

    first_messages = []
    both = []
    for k in number:
        table = after(forward_table, first_messages[-1]) if k else forward_table
        count = 16 * len(chunks[k])
        shape = (2, 4, 2, heights[k], width)
        leaving = group_products(table, tiles, source, count, 2 * k, False)
        core_in = exchange(leaving, "col", 1).reshape(shape)
        kept = group_products(table, tiles, source, count, 2 * k + 1, False).reshape(shape)

        def sums(half, low, high, kept=kept, core_in=core_in):
            return wide(kept[half, low:high]) + wide(core_in[half, low:high])

        both.append(sums)
        first_messages.append((sums(0, 1, 3).astype(bf16), sums(1, 2, 4).astype(bf16)))
    reduced = []
    second_messages = None
    all_second = []
    for k in number:
        messages = first_messages[k]
        if k:
            messages = after(messages, second_messages)
        low_in = exchange(messages[0], "col", near)
        high_in = exchange(messages[1], "col", far)
        low_in, high_in = lax.optimization_barrier((low_in, high_in))
        second_messages = (
            (both[k](0, 3, 4)[0] + wide(low_in[1])).astype(bf16),
            (both[k](1, 1, 2)[0] + wide(high_in[0])).astype(bf16),
        )
        second_messages = lax.optimization_barrier(second_messages)
        all_second.append(second_messages)
        low_next = exchange(second_messages[0], "col", far)
        high_next = exchange(second_messages[1], "col", near)
        low = both[k](0, 0, 1)[0] + wide(low_in[0]) + wide(low_next)
        high = both[k](1, 0, 1)[0] + wide(high_in[1]) + wide(high_next)
        blocks = (low[0], low[1].astype(bf16), high[0].astype(bf16), high[1].astype(bf16))
        reduced.append(after(blocks, first_messages[k + 1 :]))

    hidden_parts = []
    local_weight = jnp.zeros((width, width), f32)
    stacks = []
    upstream = None
    for k in number:
        rows = heights[k]
        last = k == len(chunks) - 1
        blocks = reduced[k]
        if k:
            blocks = after(blocks, upstream)
        summed = blocks[0]
        for distance in (1, 2, 3):
            summed = summed + wide(exchange(blocks[distance], "col", distance << z_bit))
        if k:
            summed = after(summed, stacks[-1])
        chunk_scale = own(k, scale_in)
        aggregate = (chunk_scale[:, None] * summed).astype(bf16)
        preact = jnp.dot(aggregate, weight, preferred_element_type=f32)
        gates = jax.nn.sigmoid(preact)
        hidden_parts.append((preact * gates).astype(bf16))
        delta = (wide(own(k, grad_out)) * gates * (1.0 + preact * (1.0 - gates))).astype(bf16)
        local_weight = local_weight + lax.dot_general(
            aggregate, delta, (((0,), (0,)), ((), ())), preferred_element_type=f32
        )
        projected = lax.dot_general(
            delta, weight, (((1,), (1,)), ((), ())), preferred_element_type=f32
        )
        upstream = (chunk_scale[:, None] * projected).astype(bf16)

        def weight_share(distance):
            return lax.dynamic_slice_in_dim(
                local_weight, (z ^ distance) * share_rows, share_rows, 0
            )

        stack = [upstream]
        messages = (upstream,) * 3
        if last:
            share = weight_share(0)
            messages = lax.optimization_barrier(
                tuple(
                    jnp.concatenate([upstream, weight_share(d).astype(bf16)], axis=0)
                    for d in (1, 2, 3)
                )
            )
        for distance, message in zip((1, 2, 3), messages):
            message = exchange(message, "col", distance << z_bit)
            stack.append(message[:rows])
            if last:
                share = share + wide(message[rows:])
        if last:
            stack.append(share.astype(bf16))
        stacks.append(after(jnp.concatenate(stack, axis=0), all_second[k + 1 :]))

    terms = None
    for k in number:
        rows = heights[k]
        last = k == len(chunks) - 1
        stack = stacks[k]
        if k:
            stack = after(stack, (second_low, second_high))
        first = exchange(stack, "col", near)
        third = exchange(stack, "col", far)
        if not last:
            first, third = after((first, third), messages)
        if k:
            terms = group_products(
                backward_table,
                tiles,
                arrivals(k - 1),
                n_row * per_owner,
                k - 1,
                True,
                terms,
                f32,
            )
            first, third = after((first, third), terms)
        low = first[: 2 * rows]
        if last:
            low = jnp.concatenate([low, first[4 * rows :]], axis=0)
        second_low = exchange(low, "col", far)
        second_high = exchange(third[2 * rows : 4 * rows], "col", near)
        if last:
            share = (wide(stack[4 * rows :]) + wide(first[4 * rows :])) + (
                wide(second_low[2 * rows :]) + wide(third[4 * rows :])
            )
        blocks = [stack[: 4 * rows], first[: 4 * rows], third[: 4 * rows]]
        seconds = [second_low[: 2 * rows], second_high]
        pieces = [
            (stack, 0, 4 * rows),
            (first, 0, 4 * rows),
            (second_low, 0, 2 * rows),
            (second_high, 0, 2 * rows),
            (third, 0, 4 * rows),
        ]

        def arrivals(k, last=last, rows=rows, pieces=pieces, blocks=blocks, seconds=seconds):
            if last:
                main = exchange(jnp.concatenate(blocks, axis=0), "col", 1)
                second, base = exchange(jnp.concatenate(seconds, axis=0), "col", 1), 0
            else:
                main = exchange(jnp.concatenate(blocks + seconds, axis=0), "col", 1)
                second, base = main, 12 * rows
            arrived = [
                (main, 0, 4 * rows),
                (main, 4 * rows, 4 * rows),
                (second, base, 2 * rows),
                (second, base + 2 * rows, 2 * rows),
                (main, 8 * rows, 4 * rows),
            ]
            return pieces + arrived

    half = n_row * per_owner // 2
    last = len(chunks) - 1
    pieces = arrivals(last)
    share = share + exchange(share, "col", 1)
    share = share + exchange(after(share, pieces[-1][0]), "row", 1)

    def final_terms(table, group, base):
        return group_products(
            table, tiles, pieces, half, group, True, terms, bf16, base
        ).reshape(4, own_rows, width)

    high = final_terms(backward_table, last, half)
    low = final_terms(after(backward_table, high[2:4]), last + 1, 0)
    source_total, share = reduce_row(low, high, share)
    share = share.astype(bf16)
    grad_weight = jnp.zeros((width, width), f32)
    for distance in (0, 1, 2, 3):
        piece = exchange(share, "col", distance << z_bit) if distance else share
        grad_weight = lax.dynamic_update_slice_in_dim(
            grad_weight, wide(piece), (z ^ distance) * share_rows, 0
        )
    grad_weight = grad_weight / math.sqrt(total_nodes)
    decay = decay_rate * jnp.sqrt(out_degree.astype(f32))
    grad_embedding = scale_out[:, None] * source_total + decay[:, None] * wide(embedding)

    hidden = jnp.concatenate(hidden_parts, axis=0)
    return (hidden, grad_embedding, grad_weight)


def solution(mesh):
    in_specs = (
        P(("col", "row"), None),
        P(),
        P(("row", "col"), None),
        P(("row", "col")),
        P(("col", "row")),
        P("row", "col", None, None, None),
        P("row", "col", None, None),
        P("row", "col"),
    )
    out_specs = (P(("row", "col"), None), P(("col", "row"), None), P())
    return jax.shard_map(
        per_device, mesh=mesh, in_specs=in_specs, out_specs=out_specs, check_vma=False
    )
```

```python
import functools
import math

import jax
import jax.numpy as jnp
from jax import lax
from jax.experimental import pallas as pl
from jax.experimental.pallas import tpu as pltpu
from jax.sharding import PartitionSpec as P

decay_rate = 0.01
f32 = jnp.float32
bf16 = jnp.bfloat16

chunks = ((0,), (1, 2))
forward_unroll = 8
backward_unroll = 16
padded = 256

x_bit, z_bit, y_bit = 1, 3, 1


def exchange(value, axis, mask):
    size = lax.axis_size(axis)
    return lax.ppermute(value, axis, [(i, i ^ mask) for i in range(size)])


def after(value, earlier):
    return lax.optimization_barrier((value, earlier))[0]


def group_kernel(table, tiles, *rest, spans, group, flipped, carried, base):
    unroll = backward_unroll if flipped else forward_unroll
    pieces = rest[: len(spans)]
    previous = rest[len(spans)] if carried else None
    out, source = rest[-2:]
    slots, edge, _ = tiles.shape
    row = 0
    for piece, (first, span) in zip(pieces, spans):

        def move(i, _, piece=piece, row=row, first=first):
            source[pl.ds(row + i * 64, 64)] = piece[pl.ds(first + i * 64, 64)]
            return 0

        lax.fori_loop(0, span // 64, move, 0)
        row += span

    def clear(i, _):
        if carried:
            out[i] = previous[base + i].astype(out.dtype)
        else:
            out[i] = jnp.zeros(out.shape[1:], out.dtype)
        return 0

    lax.fori_loop(0, out.shape[0], clear, 0)
    start = table[0, slots + group]
    stop = table[0, slots + group + 1]
    dims = (((0,), (0,)), ((), ())) if flipped else (((1,), (0,)), ((), ()))

    def advance(number, total):
        for step in range(unroll):
            index = start + number * unroll + step
            real = index < stop
            entry = table[0, jnp.minimum(index, stop - 1)]
            slot = entry & 255
            place = (entry >> 8) & 255
            origin = pl.multiple_of(((entry >> 16) & 255) * edge, edge)
            fresh = jnp.logical_and(real, (entry >> 24) == 1)
            product = lax.dot_general(
                tiles[slot], source[pl.ds(origin, edge)], dims, preferred_element_type=f32
            )
            product = product * real.astype(f32)
            if carried:
                total = jnp.where(fresh, previous[place], total) + product
            else:
                total = total * (1.0 - fresh.astype(f32)) + product
            out[place - base] = total.astype(out.dtype)
        return total

    steps = (stop - start + unroll - 1) // unroll
    lax.fori_loop(0, steps, advance, jnp.zeros(out.shape[1:], f32))


def group_products(
    table, tiles, pieces, count, group, flipped, previous=None, dtype=bf16, base=0
):
    slots, edge, _ = tiles.shape
    arrays = [array for array, _, _ in pieces]
    spans = [(first, span) for _, first, span in pieces]
    width = arrays[0].shape[1]
    operands = [table, tiles] + arrays + ([] if previous is None else [previous])
    whole = pl.BlockSpec(memory_space=pltpu.VMEM)
    return pl.pallas_call(
        functools.partial(
            group_kernel,
            spans=spans,
            group=group,
            flipped=flipped,
            carried=previous is not None,
            base=base,
        ),
        out_shape=jax.ShapeDtypeStruct((count, edge, width), dtype),
        in_specs=[pl.BlockSpec(memory_space=pltpu.SMEM)] + [whole] * (len(operands) - 1),
        out_specs=whole,
        scratch_shapes=[pltpu.VMEM((sum(span for _, span in spans), width), bf16)],
        compiler_params=pltpu.CompilerParams(vmem_limit_bytes=8 << 20),
        cost_estimate=pl.CostEstimate(
            flops=2 * slots * edge * edge * width * 200 // 4,
            bytes_accessed=count * edge * width * 4 * 200,
            transcendentals=0,
        ),
        name=("backward" if flipped else "forward") + str(group),
    )(*operands)


def order_kernel(coords, place_info, tiles, forward, backward, *, per_owner):
    del tiles
    slots = coords.shape[0]
    shape = (slots, padded)
    own_col = place_info[0]
    own_row = place_info[1]
    live_count = place_info[2]
    number = lax.broadcasted_iota(jnp.int32, (slots, 1), 0)
    alive = number < live_count
    tile_row = coords[:, 0:1]
    tile_col = coords[:, 1:2]
    owner_row = ((tile_row.astype(f32) + 0.5) * (1.0 / per_owner)).astype(jnp.int32)
    owner_col = ((tile_col.astype(f32) + 0.5) * (1.0 / per_owner)).astype(jnp.int32)
    apart = owner_row ^ own_col
    part = tile_row - owner_row * per_owner
    core = apart & 1
    x = (apart >> x_bit) & 3
    z = (apart >> z_bit) & 3
    block = (z >> 1) * 8 + x * 2 + (z & 1)
    chunk = jnp.zeros_like(part)
    inner = jnp.zeros_like(part)
    breadth = jnp.zeros_like(part)
    for k, members in enumerate(chunks):
        for i, member in enumerate(members):
            chunk = jnp.where(part == member, k, chunk)
            inner = jnp.where(part == member, i, inner)
            breadth = jnp.where(part == member, len(members), breadth)
    row_apart = owner_col ^ own_row
    source_place = ((row_apart & 1) * 4 + (row_apart >> y_bit)) * per_owner
    source_place = source_place + tile_col - owner_col * per_owner
    forward_place = block * breadth + inner
    forward_key = (chunk * 2 + 1 - core) * 128 + forward_place
    backward_origin = (core * 16 + x * 4 + z) * breadth + inner
    kept = jnp.logical_and(chunk == len(chunks) - 1, (row_apart & 1) == 0)
    backward_key = (chunk + kept.astype(jnp.int32)) * 128 + source_place

    lane = lax.broadcasted_iota(jnp.int32, shape, 1)
    sub = lax.broadcasted_iota(jnp.int32, shape, 0)
    limit = ((lane[0:1] - slots) * 128).astype(f32)
    lane_number = lane[0:1].astype(f32)

    def table(key, place, origin, groups, out):
        key = jnp.where(alive, key, 1 << 20).astype(f32)
        place = jnp.where(alive, place, 0)
        origin = jnp.where(alive, origin, 0)
        across = jnp.sum(jnp.where(lane == sub, key, 0.0), axis=0, keepdims=True)
        same = jnp.logical_and(across == key, lane < sub)
        ahead = jnp.logical_and(jnp.logical_or(across < key, same), lane < slots)
        rank = jnp.sum(jnp.where(ahead, 1.0, 0.0), axis=1, keepdims=True)
        repeats = jnp.sum(jnp.where(same, 1.0, 0.0), axis=1, keepdims=True)
        fresh = (repeats == 0.0).astype(jnp.int32)
        low = (number | (place << 8)).astype(f32)
        high = (origin | (fresh << 8)).astype(f32)
        hit = rank == lane_number
        low = jnp.sum(jnp.where(hit, low, 0.0), axis=0, keepdims=True).astype(jnp.int32)
        high = jnp.sum(jnp.where(hit, high, 0.0), axis=0, keepdims=True).astype(jnp.int32)
        bound = jnp.minimum(limit, groups * 128.0)
        bounds = jnp.sum(jnp.where(key < bound, 1.0, 0.0), axis=0, keepdims=True)
        out[...] = jnp.where(lane[0:1] < slots, low | (high << 16), bounds.astype(jnp.int32))

    table(forward_key, forward_place, source_place, 2 * len(chunks), forward)
    table(backward_key, source_place, backward_origin, len(chunks) + 1, backward)


def slot_tables(coords, live_count, own_col, own_row, per_owner, tiles):
    place_info = jnp.stack([own_col, own_row, live_count])
    whole = pl.BlockSpec(memory_space=pltpu.VMEM)
    result = jax.ShapeDtypeStruct((1, padded), jnp.int32)
    return pl.pallas_call(
        functools.partial(order_kernel, per_owner=per_owner),
        out_shape=(result, result),
        in_specs=[whole, pl.BlockSpec(memory_space=pltpu.SMEM), whole],
        out_specs=(whole, whole),
        compiler_params=pltpu.CompilerParams(vmem_limit_bytes=8 << 20),
        name="order",
    )(coords, place_info, tiles)


def gather_row(block):
    near, far = 1 << y_bit, 3 << y_bit
    rows = block.shape[0]
    half = rows // 2
    across = exchange(block, "row", 1)
    first, third = exchange(block, "row", near), exchange(block, "row", far)
    first_across, third_across = exchange(across, "row", near), exchange(across, "row", far)
    low = jnp.concatenate([first[:half], first_across[:half]], axis=0)
    high = jnp.concatenate([third[half:], third_across[half:]], axis=0)
    messages = lax.optimization_barrier((low, high))
    low = exchange(messages[0], "row", far)
    high = exchange(messages[1], "row", near)
    return messages, [
        (block, 0, rows),
        (first, 0, rows),
        (low, 0, half),
        (high, 0, half),
        (third, 0, rows),
        (across, 0, rows),
        (first_across, 0, rows),
        (low, half, half),
        (high, half, half),
        (third_across, 0, rows),
    ]


def wide(value):
    return value.astype(f32)


def reduce_row(low, high, share):
    near, far = 1 << y_bit, 3 << y_bit
    width = low.shape[2]

    def send(value, mask):
        rounded = share.astype(bf16)
        message = jnp.concatenate([value.reshape(-1, width), rounded], axis=0)
        message = exchange(message, "row", mask)
        split = message.shape[0] - share.shape[0]
        return message[:split].reshape(value.shape), wide(rounded) + wide(message[split:])

    high_in, share = send(high[2:4], far)
    low_in = exchange(low[1:3], "row", near)
    high_second = (wide(high[1]) + wide(high_in[0])).astype(bf16)
    high_next, share = send(high_second, near)
    low_second = (wide(low[3]) + wide(low_in[1])).astype(bf16)
    low_next = exchange(after(low_second, high_second), "row", far)
    leaving = (wide(high[0]) + wide(high_in[1]) + wide(high_next)).astype(bf16)
    arrived = exchange(leaving, "row", 1)
    return wide(low[0]) + wide(low_in[0]) + wide(low_next) + wide(arrived), share


def per_device(
    embedding, weight, grad_out, in_degree, out_degree, tile_edges, tile_coords, tile_count
):
    tiles = tile_edges[0, 0]
    n_row = lax.axis_size("row")
    n_col = lax.axis_size("col")
    own_row = lax.axis_index("row").astype(jnp.int32)
    own_col = lax.axis_index("col").astype(jnp.int32)
    own_rows, width = embedding.shape
    edge = tiles.shape[1]
    per_owner = own_rows // edge
    total_nodes = own_rows * n_row * n_col

    scale_out = lax.rsqrt(out_degree.astype(f32))
    scale_in = lax.rsqrt(in_degree.astype(f32))
    scaled = (scale_out[:, None] * wide(embedding)).astype(bf16)
    messages, source = gather_row(scaled)
    coords = after(tile_coords[0, 0], messages)
    forward_table, backward_table = slot_tables(
        coords, tile_count[0, 0], own_col, own_row, per_owner, tiles
    )

    near, far = 1 << x_bit, 3 << x_bit
    z = (own_col >> z_bit) & 3
    share_rows = width // 4
    number = range(len(chunks))
    heights = [len(members) * edge for members in chunks]

    def own(k, value):
        return jnp.concatenate([value[m * edge : (m + 1) * edge] for m in chunks[k]], axis=0)

    first_messages = []
    both = []
    for k in number:
        table = after(forward_table, first_messages[-1]) if k else forward_table
        count = 16 * len(chunks[k])
        shape = (2, 4, 2, heights[k], width)
        leaving = group_products(table, tiles, source, count, 2 * k, False)
        core_in = exchange(leaving, "col", 1).reshape(shape)
        kept = group_products(table, tiles, source, count, 2 * k + 1, False).reshape(shape)

        def sums(half, low, high, kept=kept, core_in=core_in):
            return wide(kept[half, low:high]) + wide(core_in[half, low:high])

        both.append(sums)
        first_messages.append((sums(0, 1, 3).astype(bf16), sums(1, 2, 4).astype(bf16)))
    reduced = []
    second_messages = None
    all_second = []
    for k in number:
        messages = first_messages[k]
        if k:
            messages = after(messages, second_messages)
        low_in = exchange(messages[0], "col", near)
        high_in = exchange(messages[1], "col", far)
        low_in, high_in = lax.optimization_barrier((low_in, high_in))
        second_messages = (
            (both[k](0, 3, 4)[0] + wide(low_in[1])).astype(bf16),
            (both[k](1, 1, 2)[0] + wide(high_in[0])).astype(bf16),
        )
        second_messages = lax.optimization_barrier(second_messages)
        all_second.append(second_messages)
        low_next = exchange(second_messages[0], "col", far)
        high_next = exchange(second_messages[1], "col", near)
        low = both[k](0, 0, 1)[0] + wide(low_in[0]) + wide(low_next)
        high = both[k](1, 0, 1)[0] + wide(high_in[1]) + wide(high_next)
        blocks = (low[0], low[1].astype(bf16), high[0].astype(bf16), high[1].astype(bf16))
        reduced.append(after(blocks, first_messages[k + 1 :]))

    hidden_parts = []
    local_weight = jnp.zeros((width, width), f32)
    stacks = []
    upstream = None
    for k in number:
        rows = heights[k]
        last = k == len(chunks) - 1
        blocks = reduced[k]
        if k:
            blocks = after(blocks, upstream)
        summed = blocks[0]
        for distance in (1, 2, 3):
            summed = summed + wide(exchange(blocks[distance], "col", distance << z_bit))
        if k:
            summed = after(summed, stacks[-1])
        chunk_scale = own(k, scale_in)
        aggregate = (chunk_scale[:, None] * summed).astype(bf16)
        preact = jnp.dot(aggregate, weight, preferred_element_type=f32)
        gates = jax.nn.sigmoid(preact)
        hidden_parts.append((preact * gates).astype(bf16))
        delta = (wide(own(k, grad_out)) * gates * (1.0 + preact * (1.0 - gates))).astype(bf16)
        local_weight = local_weight + lax.dot_general(
            aggregate, delta, (((0,), (0,)), ((), ())), preferred_element_type=f32
        )
        projected = lax.dot_general(
            delta, weight, (((1,), (1,)), ((), ())), preferred_element_type=f32
        )
        upstream = (chunk_scale[:, None] * projected).astype(bf16)

        def weight_share(distance):
            return lax.dynamic_slice_in_dim(
                local_weight, (z ^ distance) * share_rows, share_rows, 0
            )

        stack = [upstream]
        messages = (upstream,) * 3
        if last:
            share = weight_share(0)
            messages = lax.optimization_barrier(
                tuple(
                    jnp.concatenate([upstream, weight_share(d).astype(bf16)], axis=0)
                    for d in (1, 2, 3)
                )
            )
        for distance, message in zip((1, 2, 3), messages):
            message = exchange(message, "col", distance << z_bit)
            stack.append(message[:rows])
            if last:
                share = share + wide(message[rows:])
        if last:
            stack.append(share.astype(bf16))
        stacks.append(after(jnp.concatenate(stack, axis=0), all_second[k + 1 :]))

    terms = None
    for k in number:
        rows = heights[k]
        last = k == len(chunks) - 1
        stack = stacks[k]
        if k:
            stack = after(stack, (second_low, second_high))
        first = exchange(stack, "col", near)
        third = exchange(stack, "col", far)
        if not last:
            first, third = after((first, third), messages)
        if k:
            terms = group_products(
                backward_table,
                tiles,
                arrivals(k - 1),
                n_row * per_owner,
                k - 1,
                True,
                terms,
                f32,
            )
            first, third = after((first, third), terms)
        low = first[: 2 * rows]
        if last:
            low = jnp.concatenate([low, first[4 * rows :]], axis=0)
        second_low = exchange(low, "col", far)
        second_high = exchange(third[2 * rows : 4 * rows], "col", near)
        if last:
            share = (wide(stack[4 * rows :]) + wide(first[4 * rows :])) + (
                wide(second_low[2 * rows :]) + wide(third[4 * rows :])
            )
        blocks = [stack[: 4 * rows], first[: 4 * rows], third[: 4 * rows]]
        seconds = [second_low[: 2 * rows], second_high]
        pieces = [
            (stack, 0, 4 * rows),
            (first, 0, 4 * rows),
            (second_low, 0, 2 * rows),
            (second_high, 0, 2 * rows),
            (third, 0, 4 * rows),
        ]

        def arrivals(k, last=last, rows=rows, pieces=pieces, blocks=blocks, seconds=seconds):
            if last:
                main = exchange(jnp.concatenate(blocks, axis=0), "col", 1)
                second, base = exchange(jnp.concatenate(seconds, axis=0), "col", 1), 0
            else:
                main = exchange(jnp.concatenate(blocks + seconds, axis=0), "col", 1)
                second, base = main, 12 * rows
            arrived = [
                (main, 0, 4 * rows),
                (main, 4 * rows, 4 * rows),
                (second, base, 2 * rows),
                (second, base + 2 * rows, 2 * rows),
                (main, 8 * rows, 4 * rows),
            ]
            return pieces + arrived

    half = n_row * per_owner // 2
    last = len(chunks) - 1
    pieces = arrivals(last)
    share = share + exchange(share, "col", 1)
    share = share + exchange(after(share, pieces[-1][0]), "row", 1)

    def final_terms(table, group, base):
        return group_products(
            table, tiles, pieces, half, group, True, terms, bf16, base
        ).reshape(4, own_rows, width)

    high = final_terms(backward_table, last, half)
    low = final_terms(after(backward_table, high[2:4]), last + 1, 0)
    source_total, share = reduce_row(low, high, share)
    share = share.astype(bf16)
    grad_weight = jnp.zeros((width, width), f32)
    for distance in (0, 1, 2, 3):
        piece = exchange(share, "col", distance << z_bit) if distance else share
        grad_weight = lax.dynamic_update_slice_in_dim(
            grad_weight, wide(piece), (z ^ distance) * share_rows, 0
        )
    grad_weight = grad_weight / math.sqrt(total_nodes)
    decay = decay_rate * jnp.sqrt(out_degree.astype(f32))
    grad_embedding = scale_out[:, None] * source_total + decay[:, None] * wide(embedding)

    hidden = jnp.concatenate(hidden_parts, axis=0)
    return (hidden, grad_embedding, grad_weight)


def solution(mesh):
    in_specs = (
        P(("col", "row"), None),
        P(),
        P(("row", "col"), None),
        P(("row", "col")),
        P(("col", "row")),
        P("row", "col", None, None, None),
        P("row", "col", None, None),
        P("row", "col"),
    )
    out_specs = (P(("row", "col"), None), P(("col", "row"), None), P())
    return jax.shard_map(
        per_device, mesh=mesh, in_specs=in_specs, out_specs=out_specs, check_vma=False
    )
```

```python
import functools
import math

import jax
import jax.numpy as jnp
from jax import lax
from jax.experimental import pallas as pl
from jax.experimental.pallas import tpu as pltpu
from jax.sharding import PartitionSpec as P

decay_rate = 0.01
f32 = jnp.float32
bf16 = jnp.bfloat16

chunks = ((0,), (1, 2))
forward_unroll = 8
backward_unroll = 16
padded = 256

x_bit, z_bit, y_bit = 1, 3, 1


def exchange(value, axis, mask):
    size = lax.axis_size(axis)
    return lax.ppermute(value, axis, [(i, i ^ mask) for i in range(size)])


def after(value, earlier):
    return lax.optimization_barrier((value, earlier))[0]


def group_kernel(table, tiles, *rest, spans, group, flipped, carried, base):
    unroll = backward_unroll if flipped else forward_unroll
    pieces = rest[: len(spans)]
    previous = rest[len(spans)] if carried else None
    out, source = rest[-2:]
    slots, edge, _ = tiles.shape
    row = 0
    for piece, (first, span) in zip(pieces, spans):

        def move(i, _, piece=piece, row=row, first=first):
            source[pl.ds(row + i * 64, 64)] = piece[pl.ds(first + i * 64, 64)]
            return 0

        lax.fori_loop(0, span // 64, move, 0)
        row += span

    def clear(i, _):
        if carried:
            out[i] = previous[base + i].astype(out.dtype)
        else:
            out[i] = jnp.zeros(out.shape[1:], out.dtype)
        return 0

    lax.fori_loop(0, out.shape[0], clear, 0)
    start = table[0, slots + group]
    stop = table[0, slots + group + 1]
    dims = (((0,), (0,)), ((), ())) if flipped else (((1,), (0,)), ((), ()))

    def advance(number, total):
        for step in range(unroll):
            index = start + number * unroll + step
            real = index < stop
            entry = table[0, jnp.minimum(index, stop - 1)]
            slot = entry & 255
            place = (entry >> 8) & 255
            origin = pl.multiple_of(((entry >> 16) & 255) * edge, edge)
            fresh = jnp.logical_and(real, (entry >> 24) == 1)
            product = lax.dot_general(
                tiles[slot], source[pl.ds(origin, edge)], dims, preferred_element_type=f32
            )
            product = product * real.astype(f32)
            if carried:
                total = jnp.where(fresh, previous[place], total) + product
            else:
                total = total * (1.0 - fresh.astype(f32)) + product
            out[place - base] = total.astype(out.dtype)
        return total

    steps = (stop - start + unroll - 1) // unroll
    lax.fori_loop(0, steps, advance, jnp.zeros(out.shape[1:], f32))


def group_products(
    table, tiles, pieces, count, group, flipped, previous=None, dtype=bf16, base=0
):
    slots, edge, _ = tiles.shape
    arrays = [array for array, _, _ in pieces]
    spans = [(first, span) for _, first, span in pieces]
    width = arrays[0].shape[1]
    operands = [table, tiles] + arrays + ([] if previous is None else [previous])
    whole = pl.BlockSpec(memory_space=pltpu.VMEM)
    return pl.pallas_call(
        functools.partial(
            group_kernel,
            spans=spans,
            group=group,
            flipped=flipped,
            carried=previous is not None,
            base=base,
        ),
        out_shape=jax.ShapeDtypeStruct((count, edge, width), dtype),
        in_specs=[pl.BlockSpec(memory_space=pltpu.SMEM)] + [whole] * (len(operands) - 1),
        out_specs=whole,
        scratch_shapes=[pltpu.VMEM((sum(span for _, span in spans), width), bf16)],
        compiler_params=pltpu.CompilerParams(vmem_limit_bytes=8 << 20),
        cost_estimate=pl.CostEstimate(
            flops=2 * slots * edge * edge * width * (1 if flipped else 200) // 4,
            bytes_accessed=count * edge * width * 4 * (1 if flipped else 200),
            transcendentals=0,
        ),
        name=("backward" if flipped else "forward") + str(group),
    )(*operands)


def order_kernel(coords, place_info, tiles, forward, backward, *, per_owner):
    del tiles
    slots = coords.shape[0]
    shape = (slots, padded)
    own_col = place_info[0]
    own_row = place_info[1]
    live_count = place_info[2]
    number = lax.broadcasted_iota(jnp.int32, (slots, 1), 0)
    alive = number < live_count
    tile_row = coords[:, 0:1]
    tile_col = coords[:, 1:2]
    owner_row = ((tile_row.astype(f32) + 0.5) * (1.0 / per_owner)).astype(jnp.int32)
    owner_col = ((tile_col.astype(f32) + 0.5) * (1.0 / per_owner)).astype(jnp.int32)
    apart = owner_row ^ own_col
    part = tile_row - owner_row * per_owner
    core = apart & 1
    x = (apart >> x_bit) & 3
    z = (apart >> z_bit) & 3
    block = (z >> 1) * 8 + x * 2 + (z & 1)
    chunk = jnp.zeros_like(part)
    inner = jnp.zeros_like(part)
    breadth = jnp.zeros_like(part)
    for k, members in enumerate(chunks):
        for i, member in enumerate(members):
            chunk = jnp.where(part == member, k, chunk)
            inner = jnp.where(part == member, i, inner)
            breadth = jnp.where(part == member, len(members), breadth)
    row_apart = owner_col ^ own_row
    source_place = ((row_apart & 1) * 4 + (row_apart >> y_bit)) * per_owner
    source_place = source_place + tile_col - owner_col * per_owner
    forward_place = block * breadth + inner
    forward_key = (chunk * 2 + 1 - core) * 128 + forward_place
    backward_origin = (core * 16 + x * 4 + z) * breadth + inner
    kept = jnp.logical_and(chunk == len(chunks) - 1, (row_apart & 1) == 0)
    backward_key = (chunk + kept.astype(jnp.int32)) * 128 + source_place

    lane = lax.broadcasted_iota(jnp.int32, shape, 1)
    sub = lax.broadcasted_iota(jnp.int32, shape, 0)
    limit = ((lane[0:1] - slots) * 128).astype(f32)
    lane_number = lane[0:1].astype(f32)

    def table(key, place, origin, groups, out):
        key = jnp.where(alive, key, 1 << 20).astype(f32)
        place = jnp.where(alive, place, 0)
        origin = jnp.where(alive, origin, 0)
        across = jnp.sum(jnp.where(lane == sub, key, 0.0), axis=0, keepdims=True)
        same = jnp.logical_and(across == key, lane < sub)
        ahead = jnp.logical_and(jnp.logical_or(across < key, same), lane < slots)
        rank = jnp.sum(jnp.where(ahead, 1.0, 0.0), axis=1, keepdims=True)
        repeats = jnp.sum(jnp.where(same, 1.0, 0.0), axis=1, keepdims=True)
        fresh = (repeats == 0.0).astype(jnp.int32)
        low = (number | (place << 8)).astype(f32)
        high = (origin | (fresh << 8)).astype(f32)
        hit = rank == lane_number
        low = jnp.sum(jnp.where(hit, low, 0.0), axis=0, keepdims=True).astype(jnp.int32)
        high = jnp.sum(jnp.where(hit, high, 0.0), axis=0, keepdims=True).astype(jnp.int32)
        bound = jnp.minimum(limit, groups * 128.0)
        bounds = jnp.sum(jnp.where(key < bound, 1.0, 0.0), axis=0, keepdims=True)
        out[...] = jnp.where(lane[0:1] < slots, low | (high << 16), bounds.astype(jnp.int32))

    table(forward_key, forward_place, source_place, 2 * len(chunks), forward)
    table(backward_key, source_place, backward_origin, len(chunks) + 1, backward)


def slot_tables(coords, live_count, own_col, own_row, per_owner, tiles):
    place_info = jnp.stack([own_col, own_row, live_count])
    whole = pl.BlockSpec(memory_space=pltpu.VMEM)
    result = jax.ShapeDtypeStruct((1, padded), jnp.int32)
    return pl.pallas_call(
        functools.partial(order_kernel, per_owner=per_owner),
        out_shape=(result, result),
        in_specs=[whole, pl.BlockSpec(memory_space=pltpu.SMEM), whole],
        out_specs=(whole, whole),
        compiler_params=pltpu.CompilerParams(vmem_limit_bytes=8 << 20),
        name="order",
    )(coords, place_info, tiles)


def gather_row(block):
    near, far = 1 << y_bit, 3 << y_bit
    rows = block.shape[0]
    half = rows // 2
    across = exchange(block, "row", 1)
    first, third = exchange(block, "row", near), exchange(block, "row", far)
    first_across, third_across = exchange(across, "row", near), exchange(across, "row", far)
    low = jnp.concatenate([first[:half], first_across[:half]], axis=0)
    high = jnp.concatenate([third[half:], third_across[half:]], axis=0)
    messages = lax.optimization_barrier((low, high))
    low = exchange(messages[0], "row", far)
    high = exchange(messages[1], "row", near)
    return messages, [
        (block, 0, rows),
        (first, 0, rows),
        (low, 0, half),
        (high, 0, half),
        (third, 0, rows),
        (across, 0, rows),
        (first_across, 0, rows),
        (low, half, half),
        (high, half, half),
        (third_across, 0, rows),
    ]


def wide(value):
    return value.astype(f32)


def reduce_row(low, high, share):
    near, far = 1 << y_bit, 3 << y_bit
    width = low.shape[2]

    def send(value, mask):
        rounded = share.astype(bf16)
        message = jnp.concatenate([value.reshape(-1, width), rounded], axis=0)
        message = exchange(message, "row", mask)
        split = message.shape[0] - share.shape[0]
        return message[:split].reshape(value.shape), wide(rounded) + wide(message[split:])

    high_in = exchange(high[2:4], "row", far)
    low_in, share = send(low[1:3], near)
    high_second = (wide(high[1]) + wide(high_in[0])).astype(bf16)
    high_next = exchange(high_second, "row", near)
    low_second = (wide(low[3]) + wide(low_in[1])).astype(bf16)
    low_next, share = send(after(low_second, high_second), far)
    leaving = (wide(high[0]) + wide(high_in[1]) + wide(high_next)).astype(bf16)
    arrived = exchange(leaving, "row", 1)
    total = wide(low[0]) + wide(low_in[0]) + wide(low_next) + wide(arrived)
    return total, after(share, leaving)


def per_device(
    embedding, weight, grad_out, in_degree, out_degree, tile_edges, tile_coords, tile_count
):
    tiles = tile_edges[0, 0]
    n_row = lax.axis_size("row")
    n_col = lax.axis_size("col")
    own_row = lax.axis_index("row").astype(jnp.int32)
    own_col = lax.axis_index("col").astype(jnp.int32)
    own_rows, width = embedding.shape
    edge = tiles.shape[1]
    per_owner = own_rows // edge
    total_nodes = own_rows * n_row * n_col

    scale_out = lax.rsqrt(out_degree.astype(f32))
    scale_in = lax.rsqrt(in_degree.astype(f32))
    scaled = (scale_out[:, None] * wide(embedding)).astype(bf16)
    messages, source = gather_row(scaled)
    coords = after(tile_coords[0, 0], messages)
    forward_table, backward_table = slot_tables(
        coords, tile_count[0, 0], own_col, own_row, per_owner, tiles
    )

    near, far = 1 << x_bit, 3 << x_bit
    z = (own_col >> z_bit) & 3
    share_rows = width // 4
    number = range(len(chunks))
    heights = [len(members) * edge for members in chunks]

    def own(k, value):
        return jnp.concatenate([value[m * edge : (m + 1) * edge] for m in chunks[k]], axis=0)

    first_messages = []
    both = []
    for k in number:
        table = after(forward_table, first_messages[-1]) if k else forward_table
        count = 16 * len(chunks[k])
        shape = (2, 4, 2, heights[k], width)
        leaving = group_products(table, tiles, source, count, 2 * k, False)
        core_in = exchange(leaving, "col", 1).reshape(shape)
        kept = group_products(table, tiles, source, count, 2 * k + 1, False).reshape(shape)

        def sums(half, low, high, kept=kept, core_in=core_in):
            return wide(kept[half, low:high]) + wide(core_in[half, low:high])

        both.append(sums)
        first_messages.append((sums(0, 1, 3).astype(bf16), sums(1, 2, 4).astype(bf16)))
    reduced = []
    second_messages = None
    all_second = []
    for k in number:
        messages = first_messages[k]
        if k:
            messages = after(messages, second_messages)
        low_in = exchange(messages[0], "col", near)
        high_in = exchange(messages[1], "col", far)
        low_in, high_in = lax.optimization_barrier((low_in, high_in))
        second_messages = (
            (both[k](0, 3, 4)[0] + wide(low_in[1])).astype(bf16),
            (both[k](1, 1, 2)[0] + wide(high_in[0])).astype(bf16),
        )
        second_messages = lax.optimization_barrier(second_messages)
        all_second.append(second_messages)
        low_next = exchange(second_messages[0], "col", far)
        high_next = exchange(second_messages[1], "col", near)
        low = both[k](0, 0, 1)[0] + wide(low_in[0]) + wide(low_next)
        high = both[k](1, 0, 1)[0] + wide(high_in[1]) + wide(high_next)
        blocks = (low[0], low[1].astype(bf16), high[0].astype(bf16), high[1].astype(bf16))
        reduced.append(after(blocks, first_messages[k + 1 :]))

    hidden_parts = []
    local_weight = jnp.zeros((width, width), f32)
    stacks = []
    upstream = None
    for k in number:
        rows = heights[k]
        last = k == len(chunks) - 1
        blocks = reduced[k]
        if k:
            blocks = after(blocks, upstream)
        summed = blocks[0]
        for distance in (1, 2, 3):
            summed = summed + wide(exchange(blocks[distance], "col", distance << z_bit))
        if k:
            summed = after(summed, stacks[-1])
        chunk_scale = own(k, scale_in)
        aggregate = (chunk_scale[:, None] * summed).astype(bf16)
        preact = jnp.dot(aggregate, weight, preferred_element_type=f32)
        gates = jax.nn.sigmoid(preact)
        hidden_parts.append((preact * gates).astype(bf16))
        delta = (wide(own(k, grad_out)) * gates * (1.0 + preact * (1.0 - gates))).astype(bf16)
        local_weight = local_weight + lax.dot_general(
            aggregate, delta, (((0,), (0,)), ((), ())), preferred_element_type=f32
        )
        projected = lax.dot_general(
            delta, weight, (((1,), (1,)), ((), ())), preferred_element_type=f32
        )
        upstream = (chunk_scale[:, None] * projected).astype(bf16)

        def weight_share(distance):
            return lax.dynamic_slice_in_dim(
                local_weight, (z ^ distance) * share_rows, share_rows, 0
            )

        stack = [upstream]
        messages = (upstream,) * 3
        if last:
            share = weight_share(0)
            messages = lax.optimization_barrier(
                tuple(
                    jnp.concatenate([upstream, weight_share(d).astype(bf16)], axis=0)
                    for d in (1, 2, 3)
                )
            )
        for distance, message in zip((1, 2, 3), messages):
            message = exchange(message, "col", distance << z_bit)
            stack.append(message[:rows])
            if last:
                share = share + wide(message[rows:])
        if last:
            stack.append(share.astype(bf16))
        stacks.append(after(jnp.concatenate(stack, axis=0), all_second[k + 1 :]))

    terms = None
    for k in number:
        rows = heights[k]
        last = k == len(chunks) - 1
        stack = stacks[k]
        if k:
            stack = after(stack, (second_low, second_high))
        first = exchange(stack, "col", near)
        third = exchange(stack, "col", far)
        if not last:
            first, third = after((first, third), messages)
        if k:
            terms = group_products(
                backward_table,
                tiles,
                arrivals(k - 1),
                n_row * per_owner,
                k - 1,
                True,
                terms,
                f32,
            )
            first, third = after((first, third), terms)
        low = first[: 2 * rows]
        if last:
            low = jnp.concatenate([low, first[4 * rows :]], axis=0)
        second_low = exchange(low, "col", far)
        second_high = exchange(third[2 * rows : 4 * rows], "col", near)
        if last:
            share = (wide(stack[4 * rows :]) + wide(first[4 * rows :])) + (
                wide(second_low[2 * rows :]) + wide(third[4 * rows :])
            )
        blocks = [stack[: 4 * rows], first[: 4 * rows], third[: 4 * rows]]
        seconds = [second_low[: 2 * rows], second_high]
        pieces = [
            (stack, 0, 4 * rows),
            (first, 0, 4 * rows),
            (second_low, 0, 2 * rows),
            (second_high, 0, 2 * rows),
            (third, 0, 4 * rows),
        ]

        def arrivals(k, last=last, rows=rows, pieces=pieces, blocks=blocks, seconds=seconds):
            if last:
                main = exchange(jnp.concatenate(blocks, axis=0), "col", 1)
                second, base = exchange(jnp.concatenate(seconds, axis=0), "col", 1), 0
            else:
                main = exchange(jnp.concatenate(blocks + seconds, axis=0), "col", 1)
                second, base = main, 12 * rows
            arrived = [
                (main, 0, 4 * rows),
                (main, 4 * rows, 4 * rows),
                (second, base, 2 * rows),
                (second, base + 2 * rows, 2 * rows),
                (main, 8 * rows, 4 * rows),
            ]
            return pieces + arrived

    half = n_row * per_owner // 2
    last = len(chunks) - 1
    pieces = arrivals(last)
    share = share + exchange(share, "col", 1)
    share = share + exchange(after(share, pieces[-1][0]), "row", 1)

    def final_terms(table, group, base):
        return group_products(
            table, tiles, pieces, half, group, True, terms, bf16, base
        ).reshape(4, own_rows, width)

    high = final_terms(backward_table, last, half)
    low = final_terms(after(backward_table, high[2:4]), last + 1, 0)
    source_total, share = reduce_row(low, high, share)
    share = share.astype(bf16)
    grad_weight = jnp.zeros((width, width), f32)
    for distance in (0, 1, 2, 3):
        piece = exchange(share, "col", distance << z_bit) if distance else share
        grad_weight = lax.dynamic_update_slice_in_dim(
            grad_weight, wide(piece), (z ^ distance) * share_rows, 0
        )
    grad_weight = grad_weight / math.sqrt(total_nodes)
    decay = decay_rate * jnp.sqrt(out_degree.astype(f32))
    grad_embedding = scale_out[:, None] * source_total + decay[:, None] * wide(embedding)

    hidden = jnp.concatenate(hidden_parts, axis=0)
    return (hidden, grad_embedding, grad_weight)


def solution(mesh):
    in_specs = (
        P(("col", "row"), None),
        P(),
        P(("row", "col"), None),
        P(("row", "col")),
        P(("col", "row")),
        P("row", "col", None, None, None),
        P("row", "col", None, None),
        P("row", "col"),
    )
    out_specs = (P(("row", "col"), None), P(("col", "row"), None), P())
    return jax.shard_map(
        per_device, mesh=mesh, in_specs=in_specs, out_specs=out_specs, check_vma=False
    )
```

```python
import functools
import math

import jax
import jax.numpy as jnp
from jax import lax
from jax.experimental import pallas as pl
from jax.experimental.pallas import tpu as pltpu
from jax.sharding import PartitionSpec as P

decay_rate = 0.01
f32 = jnp.float32
bf16 = jnp.bfloat16

chunks = ((0,), (1, 2))
forward_unroll = 8
backward_unroll = 16
padded = 256

x_bit, z_bit, y_bit = 1, 3, 1


def exchange(value, axis, mask):
    size = lax.axis_size(axis)
    return lax.ppermute(value, axis, [(i, i ^ mask) for i in range(size)])


def after(value, earlier):
    return lax.optimization_barrier((value, earlier))[0]


def group_kernel(table, tiles, *rest, spans, group, flipped, carried, base):
    unroll = backward_unroll if flipped else forward_unroll
    pieces = rest[: len(spans)]
    previous = rest[len(spans)] if carried else None
    out, source = rest[-2:]
    slots, edge, _ = tiles.shape
    row = 0
    for piece, (first, span) in zip(pieces, spans):

        def move(i, _, piece=piece, row=row, first=first):
            source[pl.ds(row + i * 64, 64)] = piece[pl.ds(first + i * 64, 64)]
            return 0

        lax.fori_loop(0, span // 64, move, 0)
        row += span

    def clear(i, _):
        if carried:
            out[i] = previous[base + i].astype(out.dtype)
        else:
            out[i] = jnp.zeros(out.shape[1:], out.dtype)
        return 0

    lax.fori_loop(0, out.shape[0], clear, 0)
    start = table[0, slots + group]
    stop = table[0, slots + group + 1]
    dims = (((0,), (0,)), ((), ())) if flipped else (((1,), (0,)), ((), ()))

    def advance(number, total):
        for step in range(unroll):
            index = start + number * unroll + step
            real = index < stop
            entry = table[0, jnp.minimum(index, stop - 1)]
            slot = entry & 255
            place = (entry >> 8) & 255
            origin = pl.multiple_of(((entry >> 16) & 255) * edge, edge)
            fresh = jnp.logical_and(real, (entry >> 24) == 1)
            product = lax.dot_general(
                tiles[slot], source[pl.ds(origin, edge)], dims, preferred_element_type=f32
            )
            product = product * real.astype(f32)
            if carried:
                total = jnp.where(fresh, previous[place], total) + product
            else:
                total = total * (1.0 - fresh.astype(f32)) + product
            out[place - base] = total.astype(out.dtype)
        return total

    steps = (stop - start + unroll - 1) // unroll
    lax.fori_loop(0, steps, advance, jnp.zeros(out.shape[1:], f32))


def group_products(
    table, tiles, pieces, count, group, flipped, previous=None, dtype=bf16, base=0
):
    slots, edge, _ = tiles.shape
    arrays = [array for array, _, _ in pieces]
    spans = [(first, span) for _, first, span in pieces]
    width = arrays[0].shape[1]
    operands = [table, tiles] + arrays + ([] if previous is None else [previous])
    whole = pl.BlockSpec(memory_space=pltpu.VMEM)
    return pl.pallas_call(
        functools.partial(
            group_kernel,
            spans=spans,
            group=group,
            flipped=flipped,
            carried=previous is not None,
            base=base,
        ),
        out_shape=jax.ShapeDtypeStruct((count, edge, width), dtype),
        in_specs=[pl.BlockSpec(memory_space=pltpu.SMEM)] + [whole] * (len(operands) - 1),
        out_specs=whole,
        scratch_shapes=[pltpu.VMEM((sum(span for _, span in spans), width), bf16)],
        compiler_params=pltpu.CompilerParams(vmem_limit_bytes=8 << 20),
        cost_estimate=pl.CostEstimate(
            flops=2 * slots * edge * edge * width * (1 if flipped else 200) // 4,
            bytes_accessed=count * edge * width * 4 * (1 if flipped else 200),
            transcendentals=0,
        ),
        name=("backward" if flipped else "forward") + str(group),
    )(*operands)


def order_kernel(coords, place_info, tiles, forward, backward, *, per_owner):
    del tiles
    slots = coords.shape[0]
    shape = (slots, padded)
    own_col = place_info[0]
    own_row = place_info[1]
    live_count = place_info[2]
    number = lax.broadcasted_iota(jnp.int32, (slots, 1), 0)
    alive = number < live_count
    tile_row = coords[:, 0:1]
    tile_col = coords[:, 1:2]
    owner_row = ((tile_row.astype(f32) + 0.5) * (1.0 / per_owner)).astype(jnp.int32)
    owner_col = ((tile_col.astype(f32) + 0.5) * (1.0 / per_owner)).astype(jnp.int32)
    apart = owner_row ^ own_col
    part = tile_row - owner_row * per_owner
    core = apart & 1
    x = (apart >> x_bit) & 3
    z = (apart >> z_bit) & 3
    block = (z >> 1) * 8 + x * 2 + (z & 1)
    chunk = jnp.zeros_like(part)
    inner = jnp.zeros_like(part)
    breadth = jnp.zeros_like(part)
    for k, members in enumerate(chunks):
        for i, member in enumerate(members):
            chunk = jnp.where(part == member, k, chunk)
            inner = jnp.where(part == member, i, inner)
            breadth = jnp.where(part == member, len(members), breadth)
    row_apart = owner_col ^ own_row
    source_place = ((row_apart & 1) * 4 + (row_apart >> y_bit)) * per_owner
    source_place = source_place + tile_col - owner_col * per_owner
    forward_place = block * breadth + inner
    forward_key = (chunk * 2 + 1 - core) * 128 + forward_place
    backward_origin = (core * 16 + x * 4 + z) * breadth + inner
    kept = jnp.logical_and(chunk == len(chunks) - 1, (row_apart & 1) == 0)
    backward_key = (chunk + kept.astype(jnp.int32)) * 128 + source_place

    lane = lax.broadcasted_iota(jnp.int32, shape, 1)
    sub = lax.broadcasted_iota(jnp.int32, shape, 0)
    limit = ((lane[0:1] - slots) * 128).astype(f32)
    lane_number = lane[0:1].astype(f32)

    def table(key, place, origin, groups, out):
        key = jnp.where(alive, key, 1 << 20).astype(f32)
        place = jnp.where(alive, place, 0)
        origin = jnp.where(alive, origin, 0)
        across = jnp.sum(jnp.where(lane == sub, key, 0.0), axis=0, keepdims=True)
        same = jnp.logical_and(across == key, lane < sub)
        ahead = jnp.logical_and(jnp.logical_or(across < key, same), lane < slots)
        rank = jnp.sum(jnp.where(ahead, 1.0, 0.0), axis=1, keepdims=True)
        repeats = jnp.sum(jnp.where(same, 1.0, 0.0), axis=1, keepdims=True)
        fresh = (repeats == 0.0).astype(jnp.int32)
        low = (number | (place << 8)).astype(f32)
        high = (origin | (fresh << 8)).astype(f32)
        hit = rank == lane_number
        low = jnp.sum(jnp.where(hit, low, 0.0), axis=0, keepdims=True).astype(jnp.int32)
        high = jnp.sum(jnp.where(hit, high, 0.0), axis=0, keepdims=True).astype(jnp.int32)
        bound = jnp.minimum(limit, groups * 128.0)
        bounds = jnp.sum(jnp.where(key < bound, 1.0, 0.0), axis=0, keepdims=True)
        out[...] = jnp.where(lane[0:1] < slots, low | (high << 16), bounds.astype(jnp.int32))

    table(forward_key, forward_place, source_place, 2 * len(chunks), forward)
    table(backward_key, source_place, backward_origin, len(chunks) + 1, backward)


def slot_tables(coords, live_count, own_col, own_row, per_owner, tiles):
    place_info = jnp.stack([own_col, own_row, live_count])
    whole = pl.BlockSpec(memory_space=pltpu.VMEM)
    result = jax.ShapeDtypeStruct((1, padded), jnp.int32)
    return pl.pallas_call(
        functools.partial(order_kernel, per_owner=per_owner),
        out_shape=(result, result),
        in_specs=[whole, pl.BlockSpec(memory_space=pltpu.SMEM), whole],
        out_specs=(whole, whole),
        compiler_params=pltpu.CompilerParams(vmem_limit_bytes=8 << 20),
        name="order",
    )(coords, place_info, tiles)


def gather_row(block):
    near, far = 1 << y_bit, 3 << y_bit
    rows = block.shape[0]
    half = rows // 2
    across = exchange(block, "row", 1)
    first, third = exchange(block, "row", near), exchange(block, "row", far)
    first_across, third_across = exchange(across, "row", near), exchange(across, "row", far)
    low = jnp.concatenate([first[:half], first_across[:half]], axis=0)
    high = jnp.concatenate([third[half:], third_across[half:]], axis=0)
    messages = lax.optimization_barrier((low, high))
    low = exchange(messages[0], "row", far)
    high = exchange(messages[1], "row", near)
    return messages, [
        (block, 0, rows),
        (first, 0, rows),
        (low, 0, half),
        (high, 0, half),
        (third, 0, rows),
        (across, 0, rows),
        (first_across, 0, rows),
        (low, half, half),
        (high, half, half),
        (third_across, 0, rows),
    ]


def wide(value):
    return value.astype(f32)


def reduce_row(low, high, share):
    near, far = 1 << y_bit, 3 << y_bit
    width = low.shape[2]

    def send(value, mask):
        rounded = share.astype(bf16)
        message = jnp.concatenate([value.reshape(-1, width), rounded], axis=0)
        message = exchange(message, "row", mask)
        split = message.shape[0] - share.shape[0]
        return message[:split].reshape(value.shape), wide(rounded) + wide(message[split:])

    high_in = exchange(high[2:4], "row", far)
    low_in, share = send(low[1:3], near)
    high_second = (wide(high[1]) + wide(high_in[0])).astype(bf16)
    high_next = exchange(high_second, "row", near)
    low_second = (wide(low[3]) + wide(low_in[1])).astype(bf16)
    low_next, share = send(low_second, far)
    leaving = (wide(high[0]) + wide(high_in[1]) + wide(high_next)).astype(bf16)
    arrived = exchange(leaving, "row", 1)
    total = wide(low[0]) + wide(low_in[0]) + wide(low_next) + wide(arrived)
    return total, share


def per_device(
    embedding, weight, grad_out, in_degree, out_degree, tile_edges, tile_coords, tile_count
):
    tiles = tile_edges[0, 0]
    n_row = lax.axis_size("row")
    n_col = lax.axis_size("col")
    own_row = lax.axis_index("row").astype(jnp.int32)
    own_col = lax.axis_index("col").astype(jnp.int32)
    own_rows, width = embedding.shape
    edge = tiles.shape[1]
    per_owner = own_rows // edge
    total_nodes = own_rows * n_row * n_col

    scale_out = lax.rsqrt(out_degree.astype(f32))
    scale_in = lax.rsqrt(in_degree.astype(f32))
    scaled = (scale_out[:, None] * wide(embedding)).astype(bf16)
    messages, source = gather_row(scaled)
    coords = after(tile_coords[0, 0], messages)
    forward_table, backward_table = slot_tables(
        coords, tile_count[0, 0], own_col, own_row, per_owner, tiles
    )

    near, far = 1 << x_bit, 3 << x_bit
    z = (own_col >> z_bit) & 3
    share_rows = width // 4
    number = range(len(chunks))
    heights = [len(members) * edge for members in chunks]

    def own(k, value):
        return jnp.concatenate([value[m * edge : (m + 1) * edge] for m in chunks[k]], axis=0)

    first_messages = []
    both = []
    for k in number:
        table = after(forward_table, first_messages[-1]) if k else forward_table
        count = 16 * len(chunks[k])
        shape = (2, 4, 2, heights[k], width)
        leaving = group_products(table, tiles, source, count, 2 * k, False)
        core_in = exchange(leaving, "col", 1).reshape(shape)
        kept = group_products(table, tiles, source, count, 2 * k + 1, False).reshape(shape)

        def sums(half, low, high, kept=kept, core_in=core_in):
            return wide(kept[half, low:high]) + wide(core_in[half, low:high])

        both.append(sums)
        first_messages.append((sums(0, 1, 3).astype(bf16), sums(1, 2, 4).astype(bf16)))
    reduced = []
    second_messages = None
    all_second = []
    for k in number:
        messages = first_messages[k]
        if k:
            messages = after(messages, second_messages)
        low_in = exchange(messages[0], "col", near)
        high_in = exchange(messages[1], "col", far)
        low_in, high_in = lax.optimization_barrier((low_in, high_in))
        second_messages = (
            (both[k](0, 3, 4)[0] + wide(low_in[1])).astype(bf16),
            (both[k](1, 1, 2)[0] + wide(high_in[0])).astype(bf16),
        )
        second_messages = lax.optimization_barrier(second_messages)
        all_second.append(second_messages)
        low_next = exchange(second_messages[0], "col", far)
        high_next = exchange(second_messages[1], "col", near)
        low = both[k](0, 0, 1)[0] + wide(low_in[0]) + wide(low_next)
        high = both[k](1, 0, 1)[0] + wide(high_in[1]) + wide(high_next)
        blocks = (low[0], low[1].astype(bf16), high[0].astype(bf16), high[1].astype(bf16))
        reduced.append(after(blocks, first_messages[k + 1 :]))

    hidden_parts = []
    local_weight = jnp.zeros((width, width), f32)
    stacks = []
    upstream = None
    for k in number:
        rows = heights[k]
        last = k == len(chunks) - 1
        blocks = reduced[k]
        if k:
            blocks = after(blocks, upstream)
        summed = blocks[0]
        for distance in (1, 2, 3):
            summed = summed + wide(exchange(blocks[distance], "col", distance << z_bit))
        if k:
            summed = after(summed, stacks[-1])
        chunk_scale = own(k, scale_in)
        aggregate = (chunk_scale[:, None] * summed).astype(bf16)
        preact = jnp.dot(aggregate, weight, preferred_element_type=f32)
        gates = jax.nn.sigmoid(preact)
        hidden_parts.append((preact * gates).astype(bf16))
        delta = (wide(own(k, grad_out)) * gates * (1.0 + preact * (1.0 - gates))).astype(bf16)
        local_weight = local_weight + lax.dot_general(
            aggregate, delta, (((0,), (0,)), ((), ())), preferred_element_type=f32
        )
        projected = lax.dot_general(
            delta, weight, (((1,), (1,)), ((), ())), preferred_element_type=f32
        )
        upstream = (chunk_scale[:, None] * projected).astype(bf16)

        def weight_share(distance):
            return lax.dynamic_slice_in_dim(
                local_weight, (z ^ distance) * share_rows, share_rows, 0
            )

        stack = [upstream]
        messages = (upstream,) * 3
        if last:
            share = weight_share(0)
            messages = lax.optimization_barrier(
                tuple(
                    jnp.concatenate([upstream, weight_share(d).astype(bf16)], axis=0)
                    for d in (1, 2, 3)
                )
            )
        for distance, message in zip((1, 2, 3), messages):
            message = exchange(message, "col", distance << z_bit)
            stack.append(message[:rows])
            if last:
                share = share + wide(message[rows:])
        if last:
            stack.append(share.astype(bf16))
        stacks.append(after(jnp.concatenate(stack, axis=0), all_second[k + 1 :]))

    terms = None
    for k in number:
        rows = heights[k]
        last = k == len(chunks) - 1
        stack = stacks[k]
        if k:
            stack = after(stack, (second_low, second_high))
        first = exchange(stack, "col", near)
        third = exchange(stack, "col", far)
        if not last:
            first, third = after((first, third), messages)
        if k:
            terms = group_products(
                backward_table,
                tiles,
                arrivals(k - 1),
                n_row * per_owner,
                k - 1,
                True,
                terms,
                f32,
            )
            first, third = after((first, third), terms)
        low = first[: 2 * rows]
        if last:
            low = jnp.concatenate([low, first[4 * rows :]], axis=0)
        second_low = exchange(low, "col", far)
        second_high = exchange(third[2 * rows : 4 * rows], "col", near)
        if last:
            share = (wide(stack[4 * rows :]) + wide(first[4 * rows :])) + (
                wide(second_low[2 * rows :]) + wide(third[4 * rows :])
            )
        blocks = [stack[: 4 * rows], first[: 4 * rows], third[: 4 * rows]]
        seconds = [second_low[: 2 * rows], second_high]
        pieces = [
            (stack, 0, 4 * rows),
            (first, 0, 4 * rows),
            (second_low, 0, 2 * rows),
            (second_high, 0, 2 * rows),
            (third, 0, 4 * rows),
        ]

        def arrivals(k, last=last, rows=rows, pieces=pieces, blocks=blocks, seconds=seconds):
            if last:
                main = exchange(jnp.concatenate(blocks, axis=0), "col", 1)
                second, base = exchange(jnp.concatenate(seconds, axis=0), "col", 1), 0
            else:
                main = exchange(jnp.concatenate(blocks + seconds, axis=0), "col", 1)
                second, base = main, 12 * rows
            arrived = [
                (main, 0, 4 * rows),
                (main, 4 * rows, 4 * rows),
                (second, base, 2 * rows),
                (second, base + 2 * rows, 2 * rows),
                (main, 8 * rows, 4 * rows),
            ]
            return pieces + arrived

    half = n_row * per_owner // 2
    last = len(chunks) - 1
    pieces = arrivals(last)
    share = share + exchange(share, "col", 1)
    share = share + exchange(after(share, pieces[-1][0]), "row", 1)

    def final_terms(table, group, base):
        return group_products(
            table, tiles, pieces, half, group, True, terms, bf16, base
        ).reshape(4, own_rows, width)

    high = final_terms(backward_table, last, half)
    low = final_terms(after(backward_table, high[2:4]), last + 1, 0)
    source_total, share = reduce_row(low, high, share)
    share = share.astype(bf16)
    grad_weight = jnp.zeros((width, width), f32)
    for distance in (0, 1, 2, 3):
        piece = exchange(share, "col", distance << z_bit) if distance else share
        grad_weight = lax.dynamic_update_slice_in_dim(
            grad_weight, wide(piece), (z ^ distance) * share_rows, 0
        )
    grad_weight = grad_weight / math.sqrt(total_nodes)
    decay = decay_rate * jnp.sqrt(out_degree.astype(f32))
    grad_embedding = scale_out[:, None] * source_total + decay[:, None] * wide(embedding)

    hidden = jnp.concatenate(hidden_parts, axis=0)
    return (hidden, grad_embedding, grad_weight)


def solution(mesh):
    in_specs = (
        P(("col", "row"), None),
        P(),
        P(("row", "col"), None),
        P(("row", "col")),
        P(("col", "row")),
        P("row", "col", None, None, None),
        P("row", "col", None, None),
        P("row", "col"),
    )
    out_specs = (P(("row", "col"), None), P(("col", "row"), None), P())
    return jax.shard_map(
        per_device, mesh=mesh, in_specs=in_specs, out_specs=out_specs, check_vma=False
    )
```
